512 devices in a mesh: dp: 32 (over z_hi, x, core), seq: 16 (over y, z_lo).
Axes of the slice: x: 4, y: 4, z: 16 (z_hi: 4, z_lo: 4; z = z_hi * 4 + z_lo), core: 2. Of those that a mesh axis runs over, the one named last changes fastest.
Arguments:
- section_input: bfloat16 [32, 2048, 768], P('dp', 'seq'), may hold values from -6 to 6
- conv_kernel: bfloat16 [5, 768, 768], P(None, None, 'seq'), may hold values from -0.09375 to 0.09375
- qkv_weight: bfloat16 [1536, 4608], P(None, 'seq'), may hold values from -0.15625 to 0.15625
- gain_in: float32 [768], replicated, may hold values from 0.1 to 1.9
- gain_mid: float32 [1536], replicated, may hold values from 0.1 to 1.9
- qkv_cotangent: bfloat16 [32, 1024, 4608], P('dp', None, 'seq'), may hold values from -6 to 6
Outputs:
- qkv: bfloat16 [32, 1024, 4608], P('dp', None, 'seq')
- input_grad: bfloat16 [32, 2048, 768], P('dp', 'seq')
- kernel_grad: bfloat16 [5, 768, 768], P(None, None, 'seq')
- gain_in_grad: float32 [768], replicated
- gain_mid_grad: float32 [1536], replicated
- weight_grad: bfloat16 [1536, 4608], P(None, 'seq')
The draws below stay inside these ranges and needn't reach their ends.
All inputs are finite; a program needn't handle non-finite values.
Results may differ from the reference program's by a relative error of at most 0.02.
Values may be sent and summed in bfloat16 or wider, within the bound.
A program may use at most 64 MiB of HBM per device.

```python
import math
import jax
import jax.numpy as jnp
from jax import lax

C = 768
D = 1536
TOKENS = 1024
BATCH = 32
N_SEQ = 16


def spiked(result, own_key, source, target, blocks, factor):
    owner, partner = [(jnp.arange(result.shape[position]) // (result.shape[position] // blocks)).reshape([-1 if axis == position else 1 for axis in range(result.ndim)]) for position in (source, target)]
    chosen = jax.random.permutation(own_key, blocks)[partner]
    strong = (owner == chosen) | (owner == (partner + blocks // 2) % blocks)
    return jnp.where(strong, factor * result, result)


def block_levels(rng, shape, shards, least, high):
    loudness = 1.0
    for dim, shards_of in shards:
        draws = jax.random.uniform(jax.random.fold_in(jax.random.fold_in(rng, 6), dim), (shards_of,), jnp.float32, least / len(shards), high / len(shards))
        loudness = loudness * jnp.repeat(jnp.exp(draws), shape[dim] // shards_of).reshape((-1,) + (1,) * (len(shape) - 1 - dim))
    return loudness


def normal_values(key, shape, scale, most, split=(), dtype=jnp.bfloat16):
    result = scale * jax.random.normal(key, shape, jnp.float32)
    if split:
        result = result * block_levels(key, shape, split, -0.22, 0.18)
    return jnp.clip(result, -most, most).astype(dtype)


def heavy_noise(stream_key, dims, deviation, reach, split, heavy, kind=jnp.bfloat16):
    drawn = deviation * jax.random.normal(stream_key, dims, jnp.float32)
    if split:
        drawn = drawn * block_levels(stream_key, dims, split, -0.22, 0.18)
    return jnp.clip(spiked(drawn, jax.random.fold_in(stream_key, 3), *heavy), -reach, reach).astype(kind)


def setup_inputs(seed: int = 0) -> dict:
    keys = jax.random.split(jax.random.key(seed), 7)
    return {
        "section_input": normal_values(keys[0], (BATCH, 2 * TOKENS, C), 1.0, 6.0, ((0, 32), (1, 16))),
        "conv_kernel": normal_values(keys[1], (5, C, C), (5 * C) ** -0.5, 0.09375, ((2, 16),)),
        "qkv_weight": normal_values(keys[2], (D, 3 * D), D ** -0.5, 0.15625, ((1, 16),)),
        "gain_in": jnp.clip(1.0 + 0.18 * jax.random.normal(keys[3], (C,), jnp.float32), 0.1, 1.9),
        "gain_mid": jnp.clip(1.0 + 0.18 * jax.random.normal(keys[4], (D,), jnp.float32), 0.1, 1.9),
        "qkv_cotangent": heavy_noise(keys[5], (BATCH, TOKENS, 3 * D), 1.0, 6.0, ((0, 32), (2, 16)), (2, 1, 16, 2.0)),
    }


EPS = 1e-06

def inverse_rms(values):
    return lax.rsqrt(lax.optimization_barrier(jnp.mean(values * values, axis=-1, keepdims=True)) + EPS)

def one_sequence(section_row, conv_kernel, qkv_weight, gain_in, gain_mid, cotangent_row):
    length, chans = section_row.shape
    width = 2 * chans
    half = length // 2
    cols = qkv_weight.shape[1] // N_SEQ
    xfull = section_row.astype(jnp.float32)
    rone = inverse_rms(xfull)
    aone = xfull * rone
    normed_in = (aone * gain_in).astype(jnp.bfloat16)
    padded = jnp.pad(normed_in, ((2, 2), (0, 0)))
    conv_out = jnp.zeros((length, chans), jnp.float32)
    for k in range(5):
        conv_out = conv_out + jnp.dot(padded[k:k + length], conv_kernel[k], preferred_element_type=jnp.float32)
    sig = jax.nn.sigmoid(conv_out)
    section_out = xfull + conv_out * sig
    pooled = section_out.reshape(half, width)
    rtwo = inverse_rms(pooled)
    atwo = pooled * rtwo
    normed_mid = (atwo * gain_mid).astype(jnp.bfloat16)
    qkv = jnp.dot(normed_mid, qkv_weight, preferred_element_type=jnp.float32).astype(jnp.bfloat16)
    cot = cotangent_row.astype(jnp.float32)
    parts = jnp.einsum('tsc,dsc->tsd', cot.reshape(half, N_SEQ, cols), qkv_weight.astype(jnp.float32).reshape(width, N_SEQ, cols))
    parts = lax.optimization_barrier(parts.astype(jnp.bfloat16)).astype(jnp.float32)
    mid_grad = lax.optimization_barrier(jnp.sum(parts, axis=1))
    weight_term = lax.dot_general(normed_mid, cotangent_row, (((0,), (0,)), ((), ())), preferred_element_type=jnp.float32)
    gain_mid_term = lax.optimization_barrier(jnp.sum(mid_grad * atwo, axis=0))
    gmid = gain_mid * mid_grad
    pooled_grad = rtwo * (gmid - atwo * lax.optimization_barrier(jnp.mean(gmid * atwo, axis=-1, keepdims=True)))
    section_grad = pooled_grad.reshape(length, chans)
    conv_grad = (section_grad * sig * (1.0 + conv_out * (1.0 - sig))).astype(jnp.bfloat16)
    kernel_term = jnp.stack([lax.dot_general(padded[k:k + length], conv_grad, (((0,), (0,)), ((), ())), preferred_element_type=jnp.float32) for k in range(5)])
    grad_pad = jnp.pad(conv_grad, ((2, 2), (0, 0)))
    normed_grad = jnp.zeros((length, chans), jnp.float32)
    for k in range(5):
        normed_grad = normed_grad + lax.dot_general(grad_pad[4 - k:4 - k + length], conv_kernel[k], (((1,), (1,)), ((), ())), preferred_element_type=jnp.float32)
    gain_in_term = lax.optimization_barrier(jnp.sum(normed_grad * aone, axis=0))
    hin = gain_in * normed_grad
    input_grad = (section_grad + rone * (hin - aone * lax.optimization_barrier(jnp.mean(hin * aone, axis=-1, keepdims=True)))).astype(jnp.bfloat16)
    return (qkv, input_grad, kernel_term, gain_in_term, gain_mid_term, weight_term)

def reference(section_input, conv_kernel, qkv_weight, gain_in, gain_mid, qkv_cotangent):
    chans = section_input.shape[2]
    width = 2 * chans

    def step(carry, pair):
        outputs = one_sequence(pair[0], conv_kernel, qkv_weight, gain_in, gain_mid, pair[1])
        carry = (carry[0] + outputs[2], carry[1] + outputs[3], carry[2] + outputs[4], carry[3] + outputs[5])
        return (carry, (outputs[0], outputs[1]))
    start = (jnp.zeros((5, chans, chans), jnp.float32), jnp.zeros((chans,), jnp.float32), jnp.zeros((width,), jnp.float32), jnp.zeros(qkv_weight.shape, jnp.float32))
    totals, stacked = lax.scan(step, start, (section_input, qkv_cotangent))
    scale = 1.0 / math.sqrt(BATCH * TOKENS)
    return (stacked[0], stacked[1], (totals[0] * scale).astype(jnp.bfloat16), totals[1] * scale, totals[2] * scale, (totals[3] * scale).astype(jnp.bfloat16))
```

```python
import functools
import math

import jax
import jax.numpy as jnp
from jax import lax
from jax.experimental import pallas as pl
from jax.experimental.pallas import tpu as pltpu
from jax.sharding import PartitionSpec as P

EPS = 1e-06
MESH = pl.DeviceIdType.MESH
F32 = jnp.float32
BF16 = jnp.bfloat16


def wrap4(i):
    return lax.rem(i + 8, 4)


class Place:
    def __init__(self):
        self.dp = lax.axis_index("dp")
        self.seq = lax.axis_index("seq")
        self.z_hi = self.dp // 8
        self.x = lax.rem(self.dp // 2, 4)
        self.core = lax.rem(self.dp, 2)
        self.y = self.seq // 4
        self.z = lax.rem(self.seq, 4)

    def at_seq(self, y, z):
        return (self.dp, y * 4 + z)

    def y_peer(self, step):
        return self.at_seq(wrap4(self.y + step), self.z)

    def z_peer(self, step):
        return self.at_seq(self.y, wrap4(self.z + step))

    def x_peer(self, step):
        return (self.z_hi * 8 + wrap4(self.x + step) * 2 + self.core, self.seq)

    def z_hi_peer(self, step):
        return (wrap4(self.z_hi + step) * 8 + self.x * 2 + self.core, self.seq)

    def other_core(self):
        return (self.z_hi * 8 + self.x * 2 + 1 - self.core, self.seq)


class Wire:
    def __init__(self, send_sems, recv_sems, anyone):
        self.send_sems = send_sems
        self.recv_sems = recv_sems
        self.anyone = anyone
        self.started = []
        self.names = {}

    def number(self, name):
        return self.names.setdefault(name, len(self.names))

    def send(self, name, src, dst, device):
        k = self.number(name)
        copy = pltpu.make_async_remote_copy(
            src_ref=src,
            dst_ref=dst,
            send_sem=self.send_sems.at[k],
            recv_sem=self.recv_sems.at[k],
            device_id=device,
            device_id_type=MESH,
        )
        copy.start()
        self.started.append(copy)

    def recv(self, name, ref):
        k = self.number(name)
        pltpu.make_async_remote_copy(
            src_ref=ref,
            dst_ref=ref,
            send_sem=self.send_sems.at[k],
            recv_sem=self.recv_sems.at[k],
            device_id=self.anyone,
            device_id_type=MESH,
        ).wait_recv()

    def drain(self):
        for copy in self.started:
            copy.wait_send()


def greet(peers):
    barrier = pltpu.get_barrier_semaphore()
    for peer in peers:
        pl.semaphore_signal(barrier, inc=1, device_id=peer, device_id_type=MESH)
    pl.semaphore_wait(barrier, len(peers))


class Gather:
    def __init__(self, wire, place, tag, view):
        self.wire, self.place, self.tag, self.view = wire, place, tag, view

    def column(self, step):
        return self.view(wrap4(self.place.y + step) * 4, 4)

    def start(self, src):
        p = self.place
        for d in (1, 3, 2):
            self.wire.send((self.tag, "z", d), src, self.view(p.seq, 1), p.z_peer(d))

    def own_column(self):
        p = self.place
        for d in (1, 3, 2):
            block = p.y * 4 + wrap4(p.z - d)
            self.wire.recv((self.tag, "z", d), self.view(block, 1))
        for step in (1, -1):
            mine = self.column(0)
            self.wire.send((self.tag, "y", step), mine, mine, p.y_peer(step))

    def near_columns(self):
        p = self.place
        for step, skip in ((1, 0), (-1, 2)):
            got = self.column(-step)
            self.wire.recv((self.tag, "y", step), got)
            part = self.view(wrap4(p.y - step) * 4 + skip, 2)
            self.wire.send((self.tag, "relay", step), part, part, p.y_peer(step))

    def far_column(self):
        far = wrap4(self.place.y + 2) * 4
        for step, skip in ((1, 0), (-1, 2)):
            self.wire.recv((self.tag, "relay", step), self.view(far + skip, 2))


def first_kernel(
    rows_ref, taps_ref, wt_ref, cot_ref, all_rows_ref, all_taps_ref, mid_ref,
    sums, far_send, far_recv, near_send, near_recv, column_ref, z_recv,
    send_sems, recv_sems, local_sems,
):
    p = Place()
    wire = Wire(send_sems, recv_sems, p.other_core())
    greet(
        [p.z_peer(d) for d in (1, 2, 3)]
        + [p.y_peer(1), p.y_peer(-1), p.x_peer(1), p.x_peer(-1), p.other_core()]
    )
    chans = rows_ref.shape[1]
    lanes_half = chans // 2
    lanes = pl.ds(pl.multiple_of(p.core * lanes_half, 128), lanes_half)
    tap_rows = taps_ref.shape[0]
    quarter = tap_rows // 4

    def piece_rows(x):
        return pl.ds(pl.multiple_of(x * quarter, 16), quarter)

    def taps_view(first, count):
        return all_taps_ref.at[pl.ds(first, count), piece_rows(p.x), lanes]

    def rows_view(first, count):
        return all_rows_ref.at[pl.ds(first, count)]

    taps = Gather(wire, p, "taps", taps_view)
    rows = Gather(wire, p, "rows", rows_view)
    own_taps = taps_ref.at[piece_rows(p.x), lanes]
    own_rows = rows_ref
    copies = [
        pltpu.make_async_copy(own_taps, all_taps_ref.at[p.seq, piece_rows(p.x), lanes], local_sems.at[0]),
        pltpu.make_async_copy(own_rows, all_rows_ref.at[p.seq], local_sems.at[1]),
    ]
    for d in (1, 3, 2):
        wire.send(("taps", "z", d), own_taps, all_taps_ref.at[p.seq, piece_rows(p.x), lanes], p.z_peer(d))
    for copy in copies:
        copy.start()

    length = cot_ref.shape[1] // 4
    half = length // 2
    width = wt_ref.shape[1]
    tile = 256

    def product(step, slot):
        cols = pl.ds(pl.multiple_of(wrap4(p.y + step) * length, 128), length)
        part = cot_ref[:, cols].T

        @pl.loop(0, width // tile)
        def _(n):
            span = pl.ds(pl.multiple_of(n * tile, tile), tile)
            sums[slot, :, span] = jnp.dot(part, wt_ref[:, span], preferred_element_type=F32)

    for copy in copies:
        copy.wait()
    product(2, 0)
    far_send[...] = sums[0].astype(BF16)
    wire.send("far+", far_send.at[pl.ds(0, half)], far_recv.at[0], p.y_peer(1))
    wire.send("far-", far_send.at[pl.ds(half, half)], far_recv.at[1], p.y_peer(-1))
    for d in (1, 3, 2):
        wire.send(("rows", "z", d), own_rows, all_rows_ref.at[p.seq], p.z_peer(d))
    taps.own_column()

    def x_send(step, column):
        part = taps.column(column)
        for way in (1, -1):
            wire.send(("x", way, column), part, part, p.x_peer(way))

    x_send(0, 0)
    product(1, 1)
    product(-1, 2)
    wire.recv("far+", far_recv.at[0])
    near_send[0, :half] = (sums[1, :half] + far_recv[0].astype(F32)).astype(BF16)
    near_send[0, half:] = sums[1, half:].astype(BF16)
    wire.send("near+", near_send.at[0], near_recv.at[0], p.y_peer(1))
    wire.recv("far-", far_recv.at[1])
    near_send[1, :half] = sums[2, :half].astype(BF16)
    near_send[1, half:] = (sums[2, half:] + far_recv[1].astype(F32)).astype(BF16)
    wire.send("near-", near_send.at[1], near_recv.at[1], p.y_peer(-1))
    taps.near_columns()
    x_send(0, 1)
    x_send(0, -1)
    rows.own_column()
    product(0, 0)
    taps.far_column()
    x_send(0, 2)

    def x_part(x, column):
        first = wrap4(p.y + column) * 4
        return all_taps_ref.at[pl.ds(first, 4), piece_rows(x), lanes]

    for column in (0, 1, -1, 2):
        for way in (1, -1):
            got = x_part(wrap4(p.x - way), column)
            wire.recv(("x", way, column), got)
            if (way == 1) == (column in (0, 1)):
                wire.send(("xx", column), got, got, p.x_peer(way))

    wire.recv("near+", near_recv.at[0])
    wire.recv("near-", near_recv.at[1])
    sums[0] = sums[0] + near_recv[0].astype(F32) + near_recv[1].astype(F32)
    column_ref[...] = sums[0].astype(BF16).reshape(column_ref.shape)
    for d in (1, 3, 2):
        to = wrap4(p.z + d)
        wire.send(("mid", d), column_ref.at[to], z_recv.at[d - 1], p.z_peer(d))

    def core_part(core, column):
        first = wrap4(p.y + column) * 4
        half_lanes = pl.ds(pl.multiple_of(core * lanes_half, 128), lanes_half)
        return all_taps_ref.at[pl.ds(first, 4), :, half_lanes]

    for column in (0, 1, -1, 2):
        wire.recv(("xx", column), x_part(wrap4(p.x + 2), column))
        part = core_part(p.core, column)
        wire.send(("core", column), part, part, p.other_core())
    rows.near_columns()
    for d in (1, 3, 2):
        wire.recv(("mid", d), z_recv.at[d - 1])
    block = mid_ref.shape[0]
    own = sums[0, pl.ds(pl.multiple_of(p.z * block, 8), block), :]
    mid_ref[...] = own + z_recv[0].astype(F32) + z_recv[1].astype(F32) + z_recv[2].astype(F32)
    for column in (0, 1, -1, 2):
        wire.recv(("core", column), core_part(1 - p.core, column))
    rows.far_column()
    wire.drain()


def first_call(rows, taps, wt, cot):
    shards = lax.axis_size("seq")
    length, chans = rows.shape
    width = wt.shape[1]
    column = cot.shape[1] // 4
    block = cot.shape[1] // shards
    vmem = pl.BlockSpec(memory_space=pltpu.VMEM)
    return pl.pallas_call(
        first_kernel,
        name="first",
        out_shape=(
            jax.ShapeDtypeStruct((shards, length, chans), BF16),
            jax.ShapeDtypeStruct((shards,) + taps.shape, BF16),
            jax.ShapeDtypeStruct((block, width), F32),
        ),
        in_specs=[vmem] * 4,
        out_specs=(vmem,) * 3,
        scratch_shapes=[
            pltpu.VMEM((3, column, width), F32),
            pltpu.VMEM((column, width), BF16),
            pltpu.VMEM((2, column // 2, width), BF16),
            pltpu.VMEM((2, column, width), BF16),
            pltpu.VMEM((2, column, width), BF16),
            pltpu.VMEM((4, block, width), BF16),
            pltpu.VMEM((3, block, width), BF16),
            pltpu.SemaphoreType.DMA((48,)),
            pltpu.SemaphoreType.DMA((48,)),
            pltpu.SemaphoreType.DMA((2,)),
        ],
        compiler_params=pltpu.CompilerParams(collective_id=0, has_side_effects=True, vmem_limit_bytes=60 << 20),
    )(rows, taps, wt, cot)


def second_kernel(
    mid_ref, cols_ref, head_ref, tail_ref, all_mid_ref, all_cols_ref, before_ref, after_ref,
    send_sems, recv_sems, local_sems,
):
    p = Place()
    wire = Wire(send_sems, recv_sems, p.other_core())
    shards = all_mid_ref.shape[0]

    def seq_peer(d):
        return (p.dp, lax.rem(p.seq + d, shards))

    greet([seq_peer(d) for d in range(1, shards)])
    mid = Gather(wire, p, "mid", lambda first, count: all_mid_ref.at[pl.ds(first, count)])
    for d in (1, 3, 2):
        wire.send(("mid", "z", d), mid_ref, all_mid_ref.at[p.seq], p.z_peer(d))
    own = cols_ref.shape[0] // shards

    def owned(j):
        return cols_ref.at[pl.ds(pl.multiple_of(j * own, 16), own)]

    copies = [
        pltpu.make_async_copy(mid_ref, all_mid_ref.at[p.seq], local_sems.at[0]),
        pltpu.make_async_copy(owned(p.seq), all_cols_ref.at[p.seq], local_sems.at[1]),
    ]
    for copy in copies:
        copy.start()
    wire.send("tail", tail_ref, before_ref, seq_peer(1))
    wire.send("head", head_ref, after_ref, seq_peer(shards - 1))
    for d in range(1, shards):
        wire.send(("cols", d), owned(lax.rem(p.seq + d, shards)), all_cols_ref.at[p.seq], seq_peer(d))
    for copy in copies:
        copy.wait()
    mid.own_column()
    mid.near_columns()
    wire.recv("tail", before_ref)
    wire.recv("head", after_ref)
    for d in range(1, shards):
        wire.recv(("cols", d), all_cols_ref.at[lax.rem(p.seq + shards - d, shards)])
    mid.far_column()
    wire.drain()


def second_call(mid, cols, head, tail):
    shards = lax.axis_size("seq")
    vmem = pl.BlockSpec(memory_space=pltpu.VMEM)
    return pl.pallas_call(
        second_kernel,
        name="second",
        out_shape=(
            jax.ShapeDtypeStruct((shards,) + mid.shape, BF16),
            jax.ShapeDtypeStruct((shards, cols.shape[0] // shards, cols.shape[1]), BF16),
            jax.ShapeDtypeStruct(head.shape, BF16),
            jax.ShapeDtypeStruct(head.shape, BF16),
        ),
        in_specs=[vmem] * 4,
        out_specs=(vmem,) * 4,
        scratch_shapes=[
            pltpu.SemaphoreType.DMA((26,)),
            pltpu.SemaphoreType.DMA((26,)),
            pltpu.SemaphoreType.DMA((2,)),
        ],
        compiler_params=pltpu.CompilerParams(collective_id=1, has_side_effects=True),
    )(mid, cols, head, tail)


def third_kernel(
    scale, sums_ref, gain_ref, out_ref, gain_out_ref,
    core_recv, core_sum, x_recv, x_sum, z_recv, gain_core, gain_send, gain_recv,
    send_sems, recv_sems,
):
    p = Place()
    wire = Wire(send_sems, recv_sems, p.other_core())
    stages = (p.x_peer, p.z_hi_peer, p.z_peer, p.y_peer)
    ways = (1, 3, 2)
    greet([p.other_core()] + [peer(d) for peer in stages for d in ways])

    wire.send("gain", gain_ref, gain_core, p.other_core())
    wire.send("core", sums_ref.at[1 - p.core], core_recv, p.other_core())

    def gain_stage(stage):
        for d in ways:
            wire.send(("gain", stage, d), gain_send.at[stage], gain_recv.at[stage, d - 1], stages[stage](d))

    def gain_sum(stage):
        total = gain_send[stage]
        for d in ways:
            wire.recv(("gain", stage, d), gain_recv.at[stage, d - 1])
            total = total + gain_recv[stage, d - 1]
        return total

    wire.recv("gain", gain_core)
    gain_send[0] = gain_ref[...] + gain_core[...]
    gain_stage(0)
    wire.recv("core", core_recv)

    def add_core(x):
        core_sum[x] = (sums_ref[p.core, x].astype(F32) + core_recv[x].astype(F32)).astype(BF16)

    for d in ways:
        to = wrap4(p.x + d)
        add_core(to)
        wire.send(("x", d), core_sum.at[to], x_recv.at[d - 1], p.x_peer(d))
    add_core(p.x)
    gain_send[1] = gain_sum(0)
    gain_stage(1)
    for d in ways:
        wire.recv(("x", d), x_recv.at[d - 1])

    def add_x(z):
        total = core_sum[p.x, z].astype(F32)
        for d in ways:
            total = total + x_recv[d - 1, z].astype(F32)
        x_sum[z] = total.astype(BF16)

    for d in (2, 1, 3):
        to = wrap4(p.z_hi + d)
        add_x(to)
        wire.send(("z", d), x_sum.at[to], z_recv.at[d - 1], p.z_hi_peer(d))
    add_x(p.z_hi)
    gain_send[2] = gain_sum(1)
    gain_stage(2)
    total = x_sum[p.z_hi].astype(F32)
    for d in ways:
        wire.recv(("z", d), z_recv.at[d - 1])
        total = total + z_recv[d - 1].astype(F32)
    out_ref[p.core, p.x, p.z_hi] = (total * scale).astype(BF16)
    mine = out_ref.at[p.core, p.x, p.z_hi]
    for d in (2, 1, 3):
        wire.send(("zz", d), mine, mine, p.z_hi_peer(d))
    gain_send[3] = gain_sum(2)
    gain_stage(3)
    for d in (1, 3, 2):
        wire.recv(("zz", d), out_ref.at[p.core, p.x, wrap4(p.z_hi - d)])
    mine = out_ref.at[p.core, p.x]
    for d in ways:
        wire.send(("xx", d), mine, mine, p.x_peer(d))
    gain_out_ref[...] = gain_sum(3) * scale
    for d in ways:
        wire.recv(("xx", d), out_ref.at[p.core, wrap4(p.x - d)])
    mine = out_ref.at[p.core]
    wire.send("cc", mine, mine, p.other_core())
    wire.recv("cc", out_ref.at[1 - p.core])
    wire.drain()


def third_call(scale, sums, gains):
    vmem = pl.BlockSpec(memory_space=pltpu.VMEM)
    blocks = sums.shape[1:]
    return pl.pallas_call(
        functools.partial(third_kernel, scale),
        name="third",
        out_shape=(
            jax.ShapeDtypeStruct(sums.shape, BF16),
            jax.ShapeDtypeStruct(gains.shape, F32),
        ),
        in_specs=[vmem] * 2,
        out_specs=(vmem,) * 2,
        scratch_shapes=[
            pltpu.VMEM(blocks, BF16),
            pltpu.VMEM(blocks, BF16),
            pltpu.VMEM((3,) + blocks[1:], BF16),
            pltpu.VMEM(blocks[1:], BF16),
            pltpu.VMEM((3,) + blocks[2:], BF16),
            pltpu.VMEM(gains.shape, F32),
            pltpu.VMEM((4,) + gains.shape, F32),
            pltpu.VMEM((4, 3) + gains.shape, F32),
            pltpu.SemaphoreType.DMA((27,)),
            pltpu.SemaphoreType.DMA((27,)),
        ],
        compiler_params=pltpu.CompilerParams(collective_id=2, has_side_effects=True),
    )(sums, gains)


def inverse_rms(values):
    return lax.rsqrt(jnp.mean(values * values, axis=-1, keepdims=True) + EPS)


def contract(a, b, dims):
    return lax.dot_general(a, b, (dims, ((), ())), preferred_element_type=F32)


def body(section_input, conv_kernel, qkv_weight, gain_in, gain_mid, qkv_cotangent):
    seq_rows = section_input[0]
    length, chans = seq_rows.shape
    half = length // 2
    width = 2 * chans
    shards = lax.axis_size("seq")
    seq = lax.axis_index("seq")
    own = conv_kernel.shape[2]
    scale = 1.0 / math.sqrt(lax.axis_size("dp") * shards * half)
    wt = qkv_weight.T
    cot = qkv_cotangent[0].T
    taps = jnp.transpose(conv_kernel, (0, 2, 1)).reshape(5 * own, chans)
    taps = jnp.pad(taps, ((0, -(5 * own) % 64), (0, 0)))

    xfull = seq_rows.astype(F32)
    rone = inverse_rms(xfull)
    aone = xfull * rone
    normed_in = (aone * gain_in).astype(BF16)
    all_in, all_taps, mid_grad = first_call(normed_in, taps, wt, cot)
    all_in = all_in.reshape(shards * length, chans)
    full = [
        all_taps[:, k * own : (k + 1) * own].reshape(chans, chans) for k in range(5)
    ]
    padded_all = jnp.pad(all_in, ((2, 2), (0, 0)))
    rows = lax.dynamic_slice_in_dim(padded_all, seq * length, length + 4, 0)
    conv_out = sum(contract(rows[k : k + length], full[k], ((1,), (1,))) for k in range(5))
    sig = jax.nn.sigmoid(conv_out)
    pooled = (xfull + conv_out * sig).reshape(half, width)
    rtwo = inverse_rms(pooled)
    atwo = pooled * rtwo
    normed_mid = (atwo * gain_mid).astype(BF16)
    gain_mid_term = jnp.sum(mid_grad * atwo, axis=0)
    gmid = gain_mid * mid_grad
    pooled_grad = rtwo * (gmid - atwo * jnp.mean(gmid * atwo, axis=-1, keepdims=True))
    section_grad = pooled_grad.reshape(length, chans)
    conv_grad = (section_grad * sig * (1.0 + conv_out * (1.0 - sig))).astype(BF16)
    all_mid, grad_cols, before, after = second_call(
        normed_mid, conv_grad.T, conv_grad[:16], conv_grad[length - 16 :]
    )
    all_mid = all_mid.reshape(shards * half, width)
    qkv_t = contract(wt, all_mid, ((1,), (1,))).astype(BF16)
    proj_t = contract(cot, all_mid, ((1,), (0,)))

    before = jnp.where(seq > 0, before[14:], jnp.zeros((2, chans), BF16))
    after = jnp.where(seq < shards - 1, after[:2], jnp.zeros((2, chans), BF16))
    grad_pad = jnp.concatenate([before, conv_grad, after], axis=0)
    normed_grad = sum(
        contract(grad_pad[4 - k : 4 - k + length], full[k], ((1,), (0,))) for k in range(5)
    )
    total = shards * length
    grad_cols = jnp.transpose(grad_cols, (1, 0, 2)).reshape(own, total)
    cols_pad = jnp.pad(grad_cols, ((0, 0), (2, 2)))
    shifted = jnp.concatenate([cols_pad[:, 4 - k : 4 - k + total] for k in range(5)], axis=0)
    kernel_t = contract(shifted, all_in, ((1,), (0,)))
    gain_in_term = jnp.sum(normed_grad * aone, axis=0)
    hin = gain_in * normed_grad
    input_grad = (
        section_grad + rone * (hin - aone * jnp.mean(hin * aone, axis=-1, keepdims=True))
    ).astype(BF16)

    lanes = 256
    parts = [kernel_t[:, i : i + lanes] for i in range(0, chans, lanes)]
    parts += [proj_t[:, i : i + lanes] for i in range(0, width, lanes)]
    used = sum(part.shape[0] for part in parts)
    block = -(-used // (32 * 16)) * 16
    parts.append(jnp.zeros((32 * block - used, lanes), F32))
    packed = jnp.concatenate(parts, axis=0).astype(BF16).reshape(2, 4, 4, block, lanes)
    gains = jnp.concatenate([gain_in_term, gain_mid_term]).reshape(-1, 128)
    gains = jnp.pad(gains, ((0, -gains.shape[0] % 8), (0, 0)))
    packed, gains = third_call(scale, packed, gains)
    packed = packed.reshape(32 * block, lanes)
    kernel_rows = kernel_t.shape[0]
    kernel_total = jnp.concatenate(
        [packed[i * kernel_rows : (i + 1) * kernel_rows] for i in range(chans // lanes)], axis=1
    )
    packed = packed[chans // lanes * kernel_rows :]
    proj_rows = proj_t.shape[0]
    proj_total = jnp.concatenate(
        [packed[i * proj_rows : (i + 1) * proj_rows] for i in range(width // lanes)], axis=1
    )
    gains = gains.reshape(-1)
    return (
        qkv_t.T[None],
        input_grad[None],
        jnp.transpose(kernel_total.reshape(5, own, chans), (0, 2, 1)),
        gains[:chans],
        gains[chans : chans + width],
        proj_total.T,
    )


def solution(mesh):
    placed = (
        P("dp", "seq", None),
        P(None, None, "seq"),
        P(None, "seq"),
        P(),
        P(),
        P("dp", None, "seq"),
    )
    return jax.shard_map(
        body,
        mesh=mesh,
        in_specs=placed,
        out_specs=(
            P("dp", None, "seq"),
            P("dp", "seq", None),
            P(None, None, "seq"),
            P(),
            P(),
            P(None, "seq"),
        ),
        check_vma=False,
    )
```

```python
import functools
import math

import jax
import jax.numpy as jnp
from jax import lax
from jax.experimental import pallas as pl
from jax.experimental.pallas import tpu as pltpu
from jax.sharding import PartitionSpec as P

EPS = 1e-06
MESH = pl.DeviceIdType.MESH
F32 = jnp.float32
BF16 = jnp.bfloat16


def wrap4(i):
    return lax.rem(i + 8, 4)


class Place:
    def __init__(self):
        self.dp = lax.axis_index("dp")
        self.seq = lax.axis_index("seq")
        self.z_hi = self.dp // 8
        self.x = lax.rem(self.dp // 2, 4)
        self.core = lax.rem(self.dp, 2)
        self.y = self.seq // 4
        self.z = lax.rem(self.seq, 4)

    def at_seq(self, y, z):
        return (self.dp, y * 4 + z)

    def y_peer(self, step):
        return self.at_seq(wrap4(self.y + step), self.z)

    def z_peer(self, step):
        return self.at_seq(self.y, wrap4(self.z + step))

    def x_peer(self, step):
        return (self.z_hi * 8 + wrap4(self.x + step) * 2 + self.core, self.seq)

    def z_hi_peer(self, step):
        return (wrap4(self.z_hi + step) * 8 + self.x * 2 + self.core, self.seq)

    def other_core(self):
        return (self.z_hi * 8 + self.x * 2 + 1 - self.core, self.seq)


class Wire:
    def __init__(self, send_sems, recv_sems, anyone):
        self.send_sems = send_sems
        self.recv_sems = recv_sems
        self.anyone = anyone
        self.started = []
        self.names = {}

    def number(self, name):
        return self.names.setdefault(name, len(self.names))

    def send(self, name, src, dst, device):
        k = self.number(name)
        copy = pltpu.make_async_remote_copy(
            src_ref=src,
            dst_ref=dst,
            send_sem=self.send_sems.at[k],
            recv_sem=self.recv_sems.at[k],
            device_id=device,
            device_id_type=MESH,
        )
        copy.start()
        self.started.append(copy)

    def recv(self, name, ref):
        k = self.number(name)
        pltpu.make_async_remote_copy(
            src_ref=ref,
            dst_ref=ref,
            send_sem=self.send_sems.at[k],
            recv_sem=self.recv_sems.at[k],
            device_id=self.anyone,
            device_id_type=MESH,
        ).wait_recv()

    def drain(self):
        for copy in self.started:
            copy.wait_send()


class Gather:
    order = (0, 1, 3, 2)

    def __init__(self, wire, place, tag, view):
        self.wire, self.place, self.tag, self.view = wire, place, tag, view

    def block(self, step, d):
        p = self.place
        return self.view(wrap4(p.y + step) * 4 + wrap4(p.z - d))

    def round_ring(self, d, src):
        for step in (1, -1):
            self.wire.send((self.tag, "y", step, d), src, self.block(0, d), self.place.y_peer(step))

    def start(self, src):
        for d in (1, 3, 2):
            self.wire.send((self.tag, "z", d), src, self.block(0, 0), self.place.z_peer(d))
        self.round_ring(0, src)

    def own(self, d):
        got = self.block(0, d)
        self.wire.recv((self.tag, "z", d), got)
        self.round_ring(d, got)

    def near(self, d):
        for step in (1, -1):
            got = self.block(-step, d)
            self.wire.recv((self.tag, "y", step, d), got)
            if (step == 1) == (d in (0, 1)):
                self.wire.send((self.tag, "relay", d), got, got, self.place.y_peer(step))

    def far(self, d):
        self.wire.recv((self.tag, "relay", d), self.block(2, d))


class Reduce:
    ways = (1, 3, 2)

    def __init__(self, wire, place, tag, rows, scale, packed, core_recv, core_sum, x_recv, x_sum, z_recv, out):
        self.wire, self.place, self.tag, self.rows, self.scale = wire, place, tag, rows, scale
        self.packed, self.core_recv, self.core_sum = packed, core_recv, core_sum
        self.x_recv, self.x_sum, self.z_recv, self.out = x_recv, x_sum, z_recv, out

    def span(self, blocks, count):
        return pl.ds(pl.multiple_of(blocks * self.rows, 16), count * self.rows)

    def core(self):
        p = self.place
        self.wire.send((self.tag, "core"), self.packed.at[self.span((1 - p.core) * 16, 16)], self.core_recv, p.other_core())

    def x(self):
        p = self.place
        self.wire.recv((self.tag, "core"), self.core_recv)

        def add(x):
            mine = self.packed[self.span(p.core * 16 + x * 4, 4), :].astype(F32)
            here = self.span(x * 4, 4)
            self.core_sum[here, :] = (mine + self.core_recv[here, :].astype(F32)).astype(BF16)

        for d in self.ways:
            to = wrap4(p.x + d)
            add(to)
            self.wire.send((self.tag, "x", d), self.core_sum.at[self.span(to * 4, 4)], self.x_recv.at[d - 1], p.x_peer(d))
        add(p.x)

    def z(self):
        p = self.place
        for d in self.ways:
            self.wire.recv((self.tag, "x", d), self.x_recv.at[d - 1])

        def add(z):
            total = self.core_sum[self.span(p.x * 4 + z, 1), :].astype(F32)
            here = self.span(z, 1)
            for d in self.ways:
                total = total + self.x_recv[d - 1, here, :].astype(F32)
            self.x_sum[here, :] = total.astype(BF16)

        for d in (2, 1, 3):
            to = wrap4(p.z_hi + d)
            add(to)
            self.wire.send((self.tag, "z", d), self.x_sum.at[self.span(to, 1)], self.z_recv.at[d - 1], p.z_hi_peer(d))
        add(p.z_hi)

    def zz(self):
        p = self.place
        total = self.x_sum[self.span(p.z_hi, 1), :].astype(F32)
        for d in self.ways:
            self.wire.recv((self.tag, "z", d), self.z_recv.at[d - 1])
            total = total + self.z_recv[d - 1].astype(F32)
        here = self.span(p.core * 16 + p.x * 4 + p.z_hi, 1)
        self.out[here, :] = (total * self.scale).astype(BF16)
        mine = self.out.at[here]
        for d in (2, 1, 3):
            self.wire.send((self.tag, "zz", d), mine, mine, p.z_hi_peer(d))

    def xx(self):
        p = self.place
        for d in self.ways:
            self.wire.recv((self.tag, "zz", d), self.out.at[self.span(p.core * 16 + p.x * 4 + wrap4(p.z_hi - d), 1)])
        mine = self.out.at[self.span(p.core * 16 + p.x * 4, 4)]
        for d in self.ways:
            self.wire.send((self.tag, "xx", d), mine, mine, p.x_peer(d))

    def cc(self):
        p = self.place
        for d in self.ways:
            self.wire.recv((self.tag, "xx", d), self.out.at[self.span(p.core * 16 + wrap4(p.x - d) * 4, 4)])
        mine = self.out.at[self.span(p.core * 16, 16)]
        self.wire.send((self.tag, "cc"), mine, mine, p.other_core())

    def end(self):
        self.wire.recv((self.tag, "cc"), self.out.at[self.span((1 - self.place.core) * 16, 16)])


class GainSum:
    ways = (1, 3, 2)

    def __init__(self, wire, place, core_recv, held, got):
        self.wire, self.core_recv, self.held, self.got = wire, core_recv, held, got
        self.place = place
        self.peers = (place.x_peer, place.z_hi_peer, place.z_peer, place.y_peer)

    def start(self, src):
        self.wire.send("gain", src, self.core_recv, self.place.other_core())

    def spread(self, stage):
        for d in self.ways:
            self.wire.send(("gain", stage, d), self.held.at[stage], self.got.at[stage, d - 1], self.peers[stage](d))

    def total(self, stage):
        value = self.held[stage]
        for d in self.ways:
            self.wire.recv(("gain", stage, d), self.got.at[stage, d - 1])
            value = value + self.got[stage, d - 1]
        return value

    def first(self, src):
        self.wire.recv("gain", self.core_recv)
        self.held[0] = src[...] + self.core_recv[...]
        self.spread(0)

    def onward(self, stage):
        self.held[stage] = self.total(stage - 1)
        self.spread(stage)


def contract(a, b, dims):
    return lax.dot_general(a, b, (dims, ((), ())), preferred_element_type=F32)


def whole_kernel(
    scale, own, x_ref, taps_ref, wt_ref, cot_ref, gain_in_ref, gain_mid_ref,
    qkv_ref, input_grad_ref, kernel_ref, proj_ref, gains_ref,
    all_rows, all_taps, all_mid, all_cols,
    ext, ext_back, halo, shifted, conv, section, atwo, rtwo, section_grad, normed_grad, cols, cols_wide, cols_shifted,
    part, sums, far_send, far_recv, near_send, near_recv, column_send, z_recv,
    pacc,
    k_packed, k_core, k_csum, k_x, k_xsum, k_z, k_out,
    p_packed, p_core, p_csum, p_x, p_xsum, p_z, p_out,
    g_own, g_core, g_held, g_got,
    send_sems, recv_sems, local_sem,
):
    p = Place()
    wire = Wire(send_sems, recv_sems, p.other_core())
    length, chans = x_ref.shape
    half = length // 2
    width = 2 * chans
    shards = all_rows.shape[0]
    nlast = shards - 1

    def seq_peer(d):
        return (p.dp, lax.rem(p.seq + d, shards))

    peers = [seq_peer(d) for d in range(1, shards)]
    peers += [p.x_peer(d) for d in (1, 2, 3)] + [p.z_hi_peer(d) for d in (1, 2, 3)] + [p.other_core()]
    barrier = pltpu.get_barrier_semaphore()
    for peer in peers:
        pl.semaphore_signal(barrier, inc=1, device_id=peer, device_id_type=MESH)

    step_rows = 32

    def chunks(body, count=length, size=step_rows):
        @pl.loop(0, count // size)
        def _(i):
            body(pl.multiple_of(i * size, size))

    def first_norm(at, size=step_rows):
        x = x_ref[pl.ds(at, size), :].astype(F32)
        r = lax.rsqrt(jnp.mean(x * x, axis=-1, keepdims=True) + EPS)
        return x, r, x * r

    def norm_rows(at):
        normed = (first_norm(at)[2] * gain_in_ref[...]).astype(BF16)
        all_rows[p.seq, pl.ds(at, step_rows), :] = normed
        ext[pl.ds(8 + at, step_rows), :] = normed.astype(F32)

    chunks(norm_rows)
    pl.semaphore_wait(barrier, len(peers))

    lanes_half = chans // 2
    quarter = taps_ref.shape[0] // 4

    def core_lanes(core):
        return pl.ds(pl.multiple_of(core * lanes_half, 128), lanes_half)

    def piece(x):
        return pl.ds(pl.multiple_of(x * quarter, 16), quarter)

    my_lanes = core_lanes(p.core)
    own_taps = taps_ref.at[piece(p.x), my_lanes]
    taps = Gather(wire, p, "taps", lambda block: all_taps.at[block, piece(p.x), my_lanes])
    rows = Gather(wire, p, "rows", lambda block: all_rows.at[block])
    mid = Gather(wire, p, "mid", lambda block: all_mid.at[block])
    taps.start(own_taps)
    local = pltpu.make_async_copy(own_taps, all_taps.at[p.seq, piece(p.x), my_lanes], local_sem.at[0])
    local.start()
    wire.send("tail", ext.at[pl.ds(length, 8)], halo.at[0], seq_peer(1))
    wire.send("head", ext.at[pl.ds(8, 8)], halo.at[1], seq_peer(nlast))

    def x_part(x, column):
        return all_taps.at[pl.ds(wrap4(p.y + column) * 4, 4), piece(x), my_lanes]

    def x_send(column):
        mine = x_part(p.x, column)
        for way in (1, -1):
            wire.send(("x", way, column), mine, mine, p.x_peer(way))

    def x_relay(column):
        for way in (1, -1):
            got = x_part(wrap4(p.x - way), column)
            wire.recv(("x", way, column), got)
            if (way == 1) == (column in (0, 1)):
                wire.send(("xx", column), got, got, p.x_peer(way))

    def core_part(core, column):
        return all_taps.at[pl.ds(wrap4(p.y + column) * 4, 4), :, core_lanes(core)]

    def core_send(column):
        wire.recv(("xx", column), x_part(wrap4(p.x + 2), column))
        mine = core_part(p.core, column)
        wire.send(("core", column), mine, mine, p.other_core())

    span_rows = cot_ref.shape[1] // 4
    span_half = span_rows // 2
    tile = 256
    slot_of = {2: 0, 1: 1, -1: 2, 0: 3}

    def column_lanes(step):
        return pl.ds(pl.multiple_of(wrap4(p.y + step) * span_rows, 128), span_rows)

    def half_lanes(h):
        return pl.ds(h * chans, chans)

    def product(step, h):
        if h == 0:
            part[...] = cot_ref[:, column_lanes(step)].T

        @pl.loop(0, chans // tile)
        def _(n):
            span = pl.ds(pl.multiple_of(h * chans + n * tile, tile), tile)
            sums[slot_of[step], :, span] = contract(part[...], wt_ref[:, span], ((1,), (0,)))

    def far_out(h):
        lanes = half_lanes(h)
        far_send[:, lanes] = sums[0, :, lanes].astype(BF16)
        wire.send(("far+", h), far_send.at[pl.ds(0, span_half), lanes], far_recv.at[0, :, lanes], p.y_peer(1))
        wire.send(("far-", h), far_send.at[pl.ds(span_half, span_half), lanes], far_recv.at[1, :, lanes], p.y_peer(-1))

    def near_out(h):
        lanes = half_lanes(h)
        wire.recv(("far+", h), far_recv.at[0, :, lanes])
        near_send[0, :span_half, lanes] = (sums[1, :span_half, lanes] + far_recv[0, :, lanes].astype(F32)).astype(BF16)
        near_send[0, span_half:, lanes] = sums[1, span_half:, lanes].astype(BF16)
        wire.send(("near+", h), near_send.at[0, :, lanes], near_recv.at[0, :, lanes], p.y_peer(1))
        wire.recv(("far-", h), far_recv.at[1, :, lanes])
        near_send[1, :span_half, lanes] = sums[2, :span_half, lanes].astype(BF16)
        near_send[1, span_half:, lanes] = (sums[2, span_half:, lanes] + far_recv[1, :, lanes].astype(F32)).astype(BF16)
        wire.send(("near-", h), near_send.at[1, :, lanes], near_recv.at[1, :, lanes], p.y_peer(-1))

    def mid_out(h):
        lanes = half_lanes(h)
        wire.recv(("near+", h), near_recv.at[0, :, lanes])
        wire.recv(("near-", h), near_recv.at[1, :, lanes])

        @pl.loop(0, 4)
        def _(i):
            at = pl.ds(pl.multiple_of(i * half, 16), half)
            total = sums[3, at, lanes] + near_recv[0, at, lanes].astype(F32) + near_recv[1, at, lanes].astype(F32)
            sums[3, at, lanes] = total
            column_send[i, :, lanes] = total.astype(BF16)

        for d in (1, 3, 2):
            wire.send(("mid", h, d), column_send.at[wrap4(p.z + d), :, lanes], z_recv.at[d - 1, :, lanes], p.z_peer(d))

    def mid_in(h):
        for d in (1, 3, 2):
            wire.recv(("mid", h, d), z_recv.at[d - 1, :, half_lanes(h)])

    product(2, 0)
    far_out(0)
    product(2, 1)
    far_out(1)
    local.wait()
    for d in (1, 3, 2):
        taps.own(d)
    x_send(0)
    product(1, 0)
    product(1, 1)
    for d in taps.order:
        taps.near(d)
    x_send(1)
    x_send(-1)
    product(-1, 0)
    product(-1, 1)
    near_out(0)
    near_out(1)
    for d in taps.order:
        taps.far(d)
    x_send(2)
    rows.start(all_rows.at[p.seq])
    product(0, 0)
    product(0, 1)
    x_relay(0)
    mid_out(0)
    for d in (1, 3, 2):
        rows.own(d)
    x_relay(1)
    core_send(0)
    x_relay(-1)
    core_send(1)
    x_relay(2)
    core_send(-1)
    mid_out(1)
    core_send(2)
    for column in (0, 1, -1, 2):
        wire.recv(("core", column), core_part(1 - p.core, column))

    def taps_of(k, group, lanes=slice(None)):
        block = all_taps[group * (shards // 2) : (group + 1) * (shards // 2), k * own : (k + 1) * own, lanes]
        return block.reshape(lanes_half, -1)

    def edges(into, recv):
        into[0:8, :] = jnp.where(p.seq > 0, recv[0], 0.0)
        into[length + 8 : length + 16, :] = jnp.where(p.seq < nlast, recv[1], 0.0)

    wire.recv("tail", halo.at[0])
    wire.recv("head", halo.at[1])
    edges(ext, halo)
    for k in range(5):
        shifted[k] = ext[6 + k : 6 + k + length, :].astype(BF16)
    for group in range(2):
        total = contract(shifted[0], taps_of(0, group), ((1,), (1,)))
        for k in range(1, 5):
            total = total + contract(shifted[k], taps_of(k, group), ((1,), (1,)))
        conv[:, group * lanes_half : (group + 1) * lanes_half] = total

    def section_rows(at):
        here = pl.ds(at, step_rows)
        c = conv[here, :]
        value = x_ref[here, :].astype(F32) + c * jax.nn.sigmoid(c)
        for j in range(chans // 128):
            section[j, here, :] = value[:, j * 128 : (j + 1) * 128]

    chunks(section_rows)
    pool_rows = 16

    def pool(i):
        at = i * pool_rows
        here = slice(at, at + pool_rows)
        even, odd = (
            jnp.concatenate(
                [section[j, pl.ds(2 * at + i, pool_rows, stride=2), :] for j in range(chans // 128)], axis=1
            )
            for i in range(2)
        )
        squares = jnp.sum(even * even, axis=-1, keepdims=True) + jnp.sum(odd * odd, axis=-1, keepdims=True)
        r = lax.rsqrt(squares / width + EPS)
        rtwo[here, :] = jnp.broadcast_to(r, (pool_rows, 128))
        for j, value in enumerate((even * r, odd * r)):
            lanes = slice(j * chans, (j + 1) * chans)
            atwo[here, lanes] = value
            all_mid[p.seq, here, lanes] = (value * gain_mid_ref[j : j + 1, :]).astype(BF16)

    for i in range(half // pool_rows):
        pool(i)
    mid.start(all_mid.at[p.seq])

    mid_in(0)
    mid_in(1)
    g_own[...] = jnp.zeros_like(g_own)

    def pool_back(i):
        at = i * pool_rows
        here = slice(at, at + pool_rows)
        r = rtwo[here, 0:1]
        grads, terms = [], 0.0
        for j in range(2):
            lanes = slice(j * chans, (j + 1) * chans)
            there = pl.ds(pl.multiple_of(p.z * half + at, 16), pool_rows)
            grad = sums[3, there, lanes]
            for d in range(3):
                grad = grad + z_recv[d, here, lanes].astype(F32)
            a = atwo[here, lanes]
            g_own[1 + j : 2 + j, :] += jnp.sum(grad * a, axis=0, keepdims=True)
            g = gain_mid_ref[j : j + 1, :] * grad
            terms = terms + jnp.sum(g * a, axis=-1, keepdims=True)
            grads.append((g, a))
        for j, (g, a) in enumerate(grads):
            value = r * (g - a * (terms / width))
            for n in range(chans // 128):
                section_grad[n, pl.ds(2 * at + j, pool_rows, stride=2), :] = value[:, n * 128 : (n + 1) * 128]

    def section_grad_rows(here):
        return jnp.concatenate([section_grad[n, here, :] for n in range(chans // 128)], axis=1)

    for i in range(half // pool_rows):
        pool_back(i)

    def conv_back(at):
        here = pl.ds(at, step_rows)
        c = conv[here, :]
        s = jax.nn.sigmoid(c)
        grad = section_grad_rows(here) * s * (1.0 + c * (1.0 - s))
        ext_back[pl.ds(8 + at, step_rows), :] = grad.astype(BF16).astype(F32)

    chunks(conv_back)
    wire.send("tail back", ext_back.at[pl.ds(length, 8)], halo.at[2], seq_peer(1))
    wire.send("head back", ext_back.at[pl.ds(8, 8)], halo.at[3], seq_peer(nlast))
    for j in range(chans // 128):
        lanes = slice(j * 128, (j + 1) * 128)
        cols[lanes, :] = ext_back[8 : 8 + length, lanes].T.astype(BF16)

    def owned(j):
        return cols.at[pl.ds(pl.multiple_of(j * own, 16), own)]

    for d in range(1, shards):
        wire.send(("cols", d), owned(lax.rem(p.seq + d, shards)), all_cols.at[p.seq], seq_peer(d))
    all_cols[p.seq] = cols[pl.ds(pl.multiple_of(p.seq * own, 16), own), :]
    mid.own(1)
    mid.own(3)
    for d in rows.order:
        rows.near(d)
    mid.own(2)

    wire.recv("tail back", halo.at[2])
    wire.recv("head back", halo.at[3])
    edges(ext_back, halo.at[pl.ds(2, 2)])
    for k in range(5):
        shifted[k] = ext_back[10 - k : 10 - k + length, :].astype(BF16)

    def through(n):
        lanes = slice(n * lanes_half, (n + 1) * lanes_half)
        total = None
        for k in range(5):
            for group in range(2):
                left = shifted[k, :, group * lanes_half : (group + 1) * lanes_half]
                term = contract(left, taps_of(k, group, lanes), ((1,), (0,)))
                total = term if total is None else total + term
        normed_grad[:, lanes] = total

    def project(step, last=False):
        block = all_mid[pl.ds(wrap4(p.y + step) * 4, 4)].reshape(span_rows, width)
        qkv_ref[:, column_lanes(step)] = contract(wt_ref[...], block, ((1,), (1,))).astype(BF16)
        left = cot_ref[:, column_lanes(step)]
        for n in range(width // tile):
            span = slice(n * tile, (n + 1) * tile)
            term = contract(left, all_mid[pl.ds(wrap4(p.y + step) * 4, 4), :, span].reshape(span_rows, tile), ((1,), (0,)))
            if step != 0:
                term = term + pacc[:, span]
            if last:
                high = term.shape[0]
                for j in range(tile // 128):
                    at = (n * (tile // 128) + j) * high
                    p_packed[at : at + high, :] = term[:, j * 128 : (j + 1) * 128].astype(BF16)
            else:
                pacc[:, span] = term

    through(0)
    mid.near(0)
    mid.near(1)
    through(1)
    mid.near(3)
    mid.near(2)

    def last_rows(at):
        here = pl.ds(at, step_rows)
        _, r, a = first_norm(at)
        grad = normed_grad[here, :]
        h = gain_in_ref[...] * grad
        g_own[0:1, :] += jnp.sum(grad * a, axis=0, keepdims=True)
        mean = jnp.mean(h * a, axis=-1, keepdims=True)
        input_grad_ref[here, :] = (section_grad_rows(here) + r * (h - a * mean)).astype(BF16)

    chunks(last_rows)
    gains = GainSum(wire, p, g_core, g_held, g_got)
    gains.start(g_own)

    for d in rows.order:
        rows.far(d)
    for d in range(1, shards):
        wire.recv(("cols", d), all_cols.at[lax.rem(p.seq + shards - d, shards)])
    for j in range(shards):
        cols_wide[:, j * length : (j + 1) * length] = all_cols[j].astype(F32)
    total_rows = shards * length
    place = lax.broadcasted_iota(jnp.int32, (own, total_rows), 1)
    for k in range(5):
        turned = cols_wide[...] if k == 2 else pltpu.roll(cols_wide[...], (k - 2) % total_rows, 1)
        source = place + (2 - k)
        turned = jnp.where((source >= 0) & (source < total_rows), turned, 0.0)
        cols_shifted[k * own : (k + 1) * own, :] = turned.astype(BF16)
    high = 5 * own
    for n in range(chans // tile):
        right = all_rows[:, :, n * tile : (n + 1) * tile].reshape(total_rows, tile)
        term = contract(cols_shifted[...], right, ((1,), (0,)))
        for j in range(tile // 128):
            at = (n * (tile // 128) + j) * high
            k_packed[at : at + high, :] = term[:, j * 128 : (j + 1) * 128].astype(BF16)

    def zero_rest(packed, used):
        packed[used:, :] = jnp.zeros((packed.shape[0] - used, 128), BF16)

    zero_rest(k_packed, high * (chans // 128))
    zero_rest(p_packed, wt_ref.shape[0] * (width // 128))
    kernel_sum = Reduce(wire, p, "k", k_z.shape[1], scale, k_packed, k_core, k_csum, k_x, k_xsum, k_z, k_out)
    proj_sum = Reduce(wire, p, "p", p_z.shape[1], scale, p_packed, p_core, p_csum, p_x, p_xsum, p_z, p_out)
    kernel_sum.core()
    gains.first(g_own)
    project(0)
    kernel_sum.x()
    project(1)
    gains.onward(1)
    kernel_sum.z()
    project(-1)
    for d in mid.order:
        mid.far(d)
    project(2, last=True)
    proj_sum.core()
    kernel_sum.zz()
    gains.onward(2)
    proj_sum.x()
    kernel_sum.xx()
    gains.onward(3)
    proj_sum.z()
    kernel_sum.cc()
    gains_ref[...] = gains.total(3) * scale
    proj_sum.zz()
    kernel_sum.end()
    for j in range(chans // 128):
        kernel_ref[:, j * 128 : (j + 1) * 128] = k_out[j * high : (j + 1) * high, :]
    proj_sum.xx()
    proj_sum.cc()
    proj_sum.end()
    high = wt_ref.shape[0]
    for j in range(width // 128):
        proj_ref[:, j * 128 : (j + 1) * 128] = p_out[j * high : (j + 1) * high, :]
    wire.drain()


def reduce_scratch(elements):
    rows = -(-elements // (128 * 32 * 16)) * 16
    shapes = ((32 * rows, 128), (16 * rows, 128), (16 * rows, 128), (3, 4 * rows, 128), (4 * rows, 128), (3, rows, 128), (32 * rows, 128))
    return [pltpu.VMEM(shape, BF16) for shape in shapes]


def body(section_input, conv_kernel, qkv_weight, gain_in, gain_mid, qkv_cotangent):
    x = section_input[0]
    length, chans = x.shape
    half = length // 2
    width = 2 * chans
    shards = lax.axis_size("seq")
    own = conv_kernel.shape[2]
    high = qkv_weight.shape[1]
    scale = 1.0 / math.sqrt(lax.axis_size("dp") * shards * half)
    taps = jnp.transpose(conv_kernel, (0, 2, 1)).reshape(5 * own, chans)
    taps = jnp.pad(taps, ((0, -(5 * own) % 64), (0, 0)))
    positions = shards * half
    column = positions // 4
    total = shards * length
    vmem = pl.BlockSpec(memory_space=pltpu.VMEM)
    gain_shape = (8, chans)
    copies = 144
    qkv, input_grad, kernel, proj, gains = pl.pallas_call(
        functools.partial(whole_kernel, scale, own),
        name="whole",
        out_shape=(
            jax.ShapeDtypeStruct((high, positions), BF16),
            jax.ShapeDtypeStruct((length, chans), BF16),
            jax.ShapeDtypeStruct((5 * own, chans), BF16),
            jax.ShapeDtypeStruct((high, width), BF16),
            jax.ShapeDtypeStruct(gain_shape, F32),
        ),
        in_specs=[vmem] * 6,
        out_specs=(vmem,) * 5,
        scratch_shapes=[
            pltpu.VMEM((shards, length, chans), BF16),
            pltpu.VMEM((shards,) + taps.shape, BF16),
            pltpu.VMEM((shards, half, width), BF16),
            pltpu.VMEM((shards, own, length), BF16),
            pltpu.VMEM((length + 16, chans), F32),
            pltpu.VMEM((length + 16, chans), F32),
            pltpu.VMEM((4, 8, chans), F32),
            pltpu.VMEM((5, length, chans), BF16),
            pltpu.VMEM((length, chans), F32),
            pltpu.VMEM((chans // 128, length, 128), F32),
            pltpu.VMEM((half, width), F32),
            pltpu.VMEM((half, 128), F32),
            pltpu.VMEM((chans // 128, length, 128), F32),
            pltpu.VMEM((length, chans), F32),
            pltpu.VMEM((chans, length), BF16),
            pltpu.VMEM((own, total), F32),
            pltpu.VMEM((5 * own, total), BF16),
            pltpu.VMEM((column, high), BF16),
            pltpu.VMEM((4, column, width), F32),
            pltpu.VMEM((column, width), BF16),
            pltpu.VMEM((2, column // 2, width), BF16),
            pltpu.VMEM((2, column, width), BF16),
            pltpu.VMEM((2, column, width), BF16),
            pltpu.VMEM((4, half, width), BF16),
            pltpu.VMEM((3, half, width), BF16),
            pltpu.VMEM((high, width), F32),
            *reduce_scratch(5 * own * chans),
            *reduce_scratch(high * width),
            pltpu.VMEM(gain_shape, F32),
            pltpu.VMEM(gain_shape, F32),
            pltpu.VMEM((4,) + gain_shape, F32),
            pltpu.VMEM((4, 3) + gain_shape, F32),
            pltpu.SemaphoreType.DMA((copies,)),
            pltpu.SemaphoreType.DMA((copies,)),
            pltpu.SemaphoreType.DMA((1,)),
        ],
        compiler_params=pltpu.CompilerParams(collective_id=0, has_side_effects=True, vmem_limit_bytes=60 << 20),
    )(x, taps, qkv_weight.T, qkv_cotangent[0].T, gain_in[None], gain_mid.reshape(2, chans))
    return (
        qkv.T[None],
        input_grad[None],
        jnp.transpose(kernel.reshape(5, own, chans), (0, 2, 1)),
        gains[0],
        gains[1:3].reshape(width),
        proj.T,
    )


def solution(mesh):
    placed = (
        P("dp", "seq", None),
        P(None, None, "seq"),
        P(None, "seq"),
        P(),
        P(),
        P("dp", None, "seq"),
    )
    return jax.shard_map(
        body,
        mesh=mesh,
        in_specs=placed,
        out_specs=(
            P("dp", None, "seq"),
            P("dp", "seq", None),
            P(None, None, "seq"),
            P(),
            P(),
            P(None, "seq"),
        ),
        check_vma=False,
    )
```

```python
import functools
import math

import jax
import jax.numpy as jnp
from jax import lax
from jax.experimental import pallas as pl
from jax.experimental.pallas import tpu as pltpu
from jax.sharding import PartitionSpec as P

EPS = 1e-06
MESH = pl.DeviceIdType.MESH
F32 = jnp.float32
BF16 = jnp.bfloat16


def wrap4(i):
    return lax.rem(i + 8, 4)


class Place:
    def __init__(self):
        self.dp = lax.axis_index("dp")
        self.seq = lax.axis_index("seq")
        self.z_hi = self.dp // 8
        self.x = lax.rem(self.dp // 2, 4)
        self.core = lax.rem(self.dp, 2)
        self.y = self.seq // 4
        self.z = lax.rem(self.seq, 4)

    def at_seq(self, y, z):
        return (self.dp, y * 4 + z)

    def y_peer(self, step):
        return self.at_seq(wrap4(self.y + step), self.z)

    def z_peer(self, step):
        return self.at_seq(self.y, wrap4(self.z + step))

    def x_peer(self, step):
        return (self.z_hi * 8 + wrap4(self.x + step) * 2 + self.core, self.seq)

    def z_hi_peer(self, step):
        return (wrap4(self.z_hi + step) * 8 + self.x * 2 + self.core, self.seq)

    def other_core(self):
        return (self.z_hi * 8 + self.x * 2 + 1 - self.core, self.seq)


class Wire:
    def __init__(self, send_sems, recv_sems, anyone):
        self.send_sems = send_sems
        self.recv_sems = recv_sems
        self.anyone = anyone
        self.started = []
        self.names = {}

    def number(self, name):
        return self.names.setdefault(name, len(self.names))

    def send(self, name, src, dst, device):
        k = self.number(name)
        copy = pltpu.make_async_remote_copy(
            src_ref=src,
            dst_ref=dst,
            send_sem=self.send_sems.at[k],
            recv_sem=self.recv_sems.at[k],
            device_id=device,
            device_id_type=MESH,
        )
        copy.start()
        self.started.append(copy)

    def recv(self, name, ref):
        k = self.number(name)
        pltpu.make_async_remote_copy(
            src_ref=ref,
            dst_ref=ref,
            send_sem=self.send_sems.at[k],
            recv_sem=self.recv_sems.at[k],
            device_id=self.anyone,
            device_id_type=MESH,
        ).wait_recv()

    def drain(self):
        for copy in self.started:
            copy.wait_send()


class Gather:
    order = (0, 1, 3, 2)

    def __init__(self, wire, place, tag, view):
        self.wire, self.place, self.tag, self.view = wire, place, tag, view

    def block(self, step, d):
        p = self.place
        return self.view(wrap4(p.y + step) * 4 + wrap4(p.z - d))

    def round_ring(self, d, src):
        for step in (1, -1):
            self.wire.send((self.tag, "y", step, d), src, self.block(0, d), self.place.y_peer(step))

    def start(self, src):
        for d in (1, 3, 2):
            self.wire.send((self.tag, "z", d), src, self.block(0, 0), self.place.z_peer(d))
        self.round_ring(0, src)

    def own(self, d):
        got = self.block(0, d)
        self.wire.recv((self.tag, "z", d), got)
        self.round_ring(d, got)

    def near(self, d):
        for step in (1, -1):
            got = self.block(-step, d)
            self.wire.recv((self.tag, "y", step, d), got)
            if (step == 1) == (d in (0, 1)):
                self.wire.send((self.tag, "relay", d), got, got, self.place.y_peer(step))

    def far(self, d):
        self.wire.recv((self.tag, "relay", d), self.block(2, d))


class Reduce:
    ways = (1, 3, 2)

    def __init__(self, wire, place, tag, rows, scale, packed, core_recv, core_sum, x_recv, x_sum, z_recv, out):
        self.wire, self.place, self.tag, self.rows, self.scale = wire, place, tag, rows, scale
        self.packed, self.core_recv, self.core_sum = packed, core_recv, core_sum
        self.x_recv, self.x_sum, self.z_recv, self.out = x_recv, x_sum, z_recv, out

    def span(self, blocks, count):
        return pl.ds(pl.multiple_of(blocks * self.rows, 16), count * self.rows)

    def core(self):
        p = self.place
        self.wire.send((self.tag, "core"), self.packed.at[self.span((1 - p.core) * 16, 16)], self.core_recv, p.other_core())

    def before_x(self):
        self.wire.recv((self.tag, "core"), self.core_recv)

    def chip_total(self, x):
        mine = self.packed[self.span(self.place.core * 16 + x * 4, 4), :].astype(F32)
        return mine + self.core_recv[self.span(x * 4, 4), :].astype(F32)

    def x(self):
        p = self.place
        self.before_x()

        def add(x):
            self.core_sum[self.span(x * 4, 4), :] = self.chip_total(x).astype(BF16)

        for d in self.ways:
            to = wrap4(p.x + d)
            add(to)
            self.wire.send((self.tag, "x", d), self.core_sum.at[self.span(to * 4, 4)], self.x_recv.at[d - 1], p.x_peer(d))
        add(p.x)

    def z(self):
        p = self.place
        for d in self.ways:
            self.wire.recv((self.tag, "x", d), self.x_recv.at[d - 1])

        def add(z):
            total = self.core_sum[self.span(p.x * 4 + z, 1), :].astype(F32)
            here = self.span(z, 1)
            for d in self.ways:
                total = total + self.x_recv[d - 1, here, :].astype(F32)
            self.x_sum[here, :] = total.astype(BF16)

        for d in (2, 1, 3):
            to = wrap4(p.z_hi + d)
            add(to)
            self.wire.send((self.tag, "z", d), self.x_sum.at[self.span(to, 1)], self.z_recv.at[d - 1], p.z_hi_peer(d))
        add(p.z_hi)

    def zz(self):
        p = self.place
        total = self.x_sum[self.span(p.z_hi, 1), :].astype(F32)
        for d in self.ways:
            self.wire.recv((self.tag, "z", d), self.z_recv.at[d - 1])
            total = total + self.z_recv[d - 1].astype(F32)
        here = self.span(p.core * 16 + p.x * 4 + p.z_hi, 1)
        self.out[here, :] = (total * self.scale).astype(BF16)
        mine = self.out.at[here]
        for d in (2, 1, 3):
            self.wire.send((self.tag, "zz", d), mine, mine, p.z_hi_peer(d))

    def xx(self):
        p = self.place
        for d in self.ways:
            self.wire.recv((self.tag, "zz", d), self.out.at[self.span(p.core * 16 + p.x * 4 + wrap4(p.z_hi - d), 1)])
        mine = self.out.at[self.span(p.core * 16 + p.x * 4, 4)]
        for d in self.ways:
            self.wire.send((self.tag, "xx", d), mine, mine, p.x_peer(d))

    def cc(self):
        p = self.place
        for d in self.ways:
            self.wire.recv((self.tag, "xx", d), self.out.at[self.span(p.core * 16 + wrap4(p.x - d) * 4, 4)])
        mine = self.out.at[self.span(p.core * 16, 16)]
        self.wire.send((self.tag, "cc"), mine, mine, p.other_core())

    def end(self):
        self.wire.recv((self.tag, "cc"), self.out.at[self.span((1 - self.place.core) * 16, 16)])


class ReduceOverY(Reduce):
    def core(self):
        p = self.place
        theirs = self.packed.at[:, self.span((1 - p.core) * 16, 16)]
        self.wire.send((self.tag, "core"), theirs, self.core_recv, p.other_core())

    def y(self, sums, got):
        p = self.place
        self.y_sums, self.y_got = sums, got
        self.wire.recv((self.tag, "core"), self.core_recv)

        def add(y):
            mine = self.packed[y, self.span(p.core * 16, 16), :].astype(F32)
            sums[y] = (mine + self.core_recv[y].astype(F32)).astype(BF16)

        for d in self.ways:
            to = wrap4(p.y + d)
            add(to)
            self.wire.send((self.tag, "y", d), sums.at[to], got.at[d - 1], p.y_peer(d))
        add(p.y)

    def before_x(self):
        for d in self.ways:
            self.wire.recv((self.tag, "y", d), self.y_got.at[d - 1])

    def chip_total(self, x):
        here = self.span(x * 4, 4)
        total = self.y_sums[self.place.y, here, :].astype(F32)
        for d in range(3):
            total = total + self.y_got[d, here, :].astype(F32)
        return total


class GainSum:
    ways = (1, 3, 2)

    def __init__(self, wire, place, core_recv, held, got):
        self.wire, self.core_recv, self.held, self.got = wire, core_recv, held, got
        self.place = place
        self.peers = (place.x_peer, place.z_hi_peer, place.z_peer, place.y_peer)

    def start(self, src):
        self.wire.send("gain", src, self.core_recv, self.place.other_core())

    def spread(self, stage):
        for d in self.ways:
            self.wire.send(("gain", stage, d), self.held.at[stage], self.got.at[stage, d - 1], self.peers[stage](d))

    def total(self, stage):
        value = self.held[stage]
        for d in self.ways:
            self.wire.recv(("gain", stage, d), self.got.at[stage, d - 1])
            value = value + self.got[stage, d - 1]
        return value

    def first(self, src):
        self.wire.recv("gain", self.core_recv)
        self.held[0] = src[...] + self.core_recv[...]
        self.spread(0)

    def onward(self, stage):
        self.held[stage] = self.total(stage - 1)
        self.spread(stage)


def contract(a, b, dims):
    return lax.dot_general(a, b, (dims, ((), ())), preferred_element_type=F32)


def whole_kernel(
    scale, own, x_ref, taps_ref, wt_ref, cot_ref, gain_in_ref, gain_mid_ref,
    qkv_ref, input_grad_ref, kernel_ref, proj_ref, gains_ref,
    line_rows, line_shifted, all_taps, all_mid, all_cols, slab,
    ext, ext_back, halo, shifted, conv, section, atwo, rtwo, section_grad, normed_grad, cols, cols_by_z,
    part, sums, far_send, far_recv, near_send, near_recv, column_send, z_recv,
    pacc,
    k_packed, k_core, k_csum, k_x, k_xsum, k_z, k_out, k_ysum, k_y,
    p_packed, p_core, p_csum, p_x, p_xsum, p_z, p_out,
    g_own, g_core, g_held, g_got,
    send_sems, recv_sems, local_sem,
):
    p = Place()
    wire = Wire(send_sems, recv_sems, p.other_core())
    length, chans = x_ref.shape
    half = length // 2
    width = 2 * chans
    shards = all_mid.shape[0]
    nlast = shards - 1

    def seq_peer(d):
        return (p.dp, lax.rem(p.seq + d, shards))

    peers = [seq_peer(1), seq_peer(nlast), p.other_core()]
    peers += [peer(d) for peer in (p.x_peer, p.y_peer, p.z_peer, p.z_hi_peer) for d in (1, 2, 3)]
    barrier = pltpu.get_barrier_semaphore()
    for peer in peers:
        pl.semaphore_signal(barrier, inc=1, device_id=peer, device_id_type=MESH)

    step_rows = 32

    def chunks(body, count=length, size=step_rows):
        @pl.loop(0, count // size)
        def _(i):
            body(pl.multiple_of(i * size, size))

    def first_norm(at, size=step_rows):
        x = x_ref[pl.ds(at, size), :].astype(F32)
        r = lax.rsqrt(jnp.mean(x * x, axis=-1, keepdims=True) + EPS)
        return x, r, x * r

    def norm_rows(at):
        normed = (first_norm(at)[2] * gain_in_ref[...]).astype(BF16)
        ext[pl.ds(8 + at, step_rows), :] = normed.astype(F32)

    chunks(norm_rows)
    pl.semaphore_wait(barrier, len(peers))

    lanes_half = chans // 2
    quarter = taps_ref.shape[0] // 4

    def core_lanes(core):
        return pl.ds(pl.multiple_of(core * lanes_half, 128), lanes_half)

    def piece(x):
        return pl.ds(pl.multiple_of(x * quarter, 16), quarter)

    my_lanes = core_lanes(p.core)
    own_taps = taps_ref.at[piece(p.x), my_lanes]
    taps = Gather(wire, p, "taps", lambda block: all_taps.at[block, piece(p.x), my_lanes])
    mid = Gather(wire, p, "mid", lambda block: all_mid.at[block])
    taps.start(own_taps)
    local = pltpu.make_async_copy(own_taps, all_taps.at[p.seq, piece(p.x), my_lanes], local_sem.at[0])
    local.start()
    wire.send("tail", ext.at[pl.ds(length, 8)], halo.at[0], seq_peer(1))
    wire.send("head", ext.at[pl.ds(8, 8)], halo.at[1], seq_peer(nlast))

    def x_part(x, column):
        return all_taps.at[pl.ds(wrap4(p.y + column) * 4, 4), piece(x), my_lanes]

    def x_send(column):
        mine = x_part(p.x, column)
        for way in (1, -1):
            wire.send(("x", way, column), mine, mine, p.x_peer(way))

    def x_relay(column):
        for way in (1, -1):
            got = x_part(wrap4(p.x - way), column)
            wire.recv(("x", way, column), got)
            if (way == 1) == (column in (0, 1)):
                wire.send(("xx", column), got, got, p.x_peer(way))

    def core_part(core, column):
        return all_taps.at[pl.ds(wrap4(p.y + column) * 4, 4), :, core_lanes(core)]

    def core_send(column):
        wire.recv(("xx", column), x_part(wrap4(p.x + 2), column))
        mine = core_part(p.core, column)
        wire.send(("core", column), mine, mine, p.other_core())

    span_rows = cot_ref.shape[1] // 4
    span_half = span_rows // 2
    tile = 256
    slot_of = {2: 0, 1: 1, -1: 2, 0: 3}

    def column_lanes(step):
        return pl.ds(pl.multiple_of(wrap4(p.y + step) * span_rows, 128), span_rows)

    def half_lanes(h):
        return pl.ds(h * chans, chans)

    def product(step, h):
        if h == 0:
            part[slot_of[step]] = cot_ref[:, column_lanes(step)].T

        @pl.loop(0, chans // tile)
        def _(n):
            span = pl.ds(pl.multiple_of(h * chans + n * tile, tile), tile)
            sums[slot_of[step], :, span] = contract(part[slot_of[step]], wt_ref[:, span], ((1,), (0,)))

    def far_out(h):
        lanes = half_lanes(h)
        far_send[:, lanes] = sums[0, :, lanes].astype(BF16)
        wire.send(("far+", h), far_send.at[pl.ds(0, span_half), lanes], far_recv.at[0, :, lanes], p.y_peer(1))
        wire.send(("far-", h), far_send.at[pl.ds(span_half, span_half), lanes], far_recv.at[1, :, lanes], p.y_peer(-1))

    def near_out(h):
        lanes = half_lanes(h)
        wire.recv(("far+", h), far_recv.at[0, :, lanes])
        near_send[0, :span_half, lanes] = (sums[1, :span_half, lanes] + far_recv[0, :, lanes].astype(F32)).astype(BF16)
        near_send[0, span_half:, lanes] = sums[1, span_half:, lanes].astype(BF16)
        wire.send(("near+", h), near_send.at[0, :, lanes], near_recv.at[0, :, lanes], p.y_peer(1))
        wire.recv(("far-", h), far_recv.at[1, :, lanes])
        near_send[1, :span_half, lanes] = sums[2, :span_half, lanes].astype(BF16)
        near_send[1, span_half:, lanes] = (sums[2, span_half:, lanes] + far_recv[1, :, lanes].astype(F32)).astype(BF16)
        wire.send(("near-", h), near_send.at[1, :, lanes], near_recv.at[1, :, lanes], p.y_peer(-1))

    def mid_out(h):
        lanes = half_lanes(h)
        wire.recv(("near+", h), near_recv.at[0, :, lanes])
        wire.recv(("near-", h), near_recv.at[1, :, lanes])

        @pl.loop(0, 4)
        def _(i):
            at = pl.ds(pl.multiple_of(i * half, 16), half)
            total = sums[3, at, lanes] + near_recv[0, at, lanes].astype(F32) + near_recv[1, at, lanes].astype(F32)
            sums[3, at, lanes] = total
            column_send[i, :, lanes] = total.astype(BF16)

        for d in (1, 3, 2):
            wire.send(("mid", h, d), column_send.at[wrap4(p.z + d), :, lanes], z_recv.at[d - 1, :, lanes], p.z_peer(d))

    def mid_in(h):
        for d in (1, 3, 2):
            wire.recv(("mid", h, d), z_recv.at[d - 1, :, half_lanes(h)])

    def edges(into, recv):
        into[0:8, :] = jnp.where(p.seq > 0, recv[0], 0.0)
        into[length + 8 : length + 16, :] = jnp.where(p.seq < nlast, recv[1], 0.0)

    product(2, 0)
    far_out(0)
    product(2, 1)
    local.wait()
    for d in (1, 3, 2):
        taps.own(d)
    x_send(0)
    far_out(1)
    wire.recv("tail", halo.at[0])
    wire.recv("head", halo.at[1])
    edges(ext, halo)
    line_rows[p.z] = ext[...].astype(BF16)
    for d in (1, 3, 2):
        wire.send(("rows", d), line_rows.at[p.z], line_rows.at[p.z], p.z_peer(d))
    for d in taps.order:
        taps.near(d)
    x_send(1)
    x_send(-1)
    product(1, 0)
    product(-1, 0)
    near_out(0)
    for d in taps.order:
        taps.far(d)
    x_send(2)
    product(1, 1)
    product(-1, 1)
    near_out(1)
    x_relay(0)
    product(0, 0)
    product(0, 1)
    x_relay(1)
    x_relay(-1)
    core_send(0)
    core_send(1)
    x_relay(2)
    mid_out(0)
    core_send(-1)
    core_send(2)
    mid_out(1)
    for k in range(5):
        shifted[k] = ext[6 + k : 6 + k + length, :].astype(BF16)
    for column in (0, 1, -1, 2):
        wire.recv(("core", column), core_part(1 - p.core, column))

    def taps_of(k, group, lanes=slice(None)):
        block = all_taps[group * (shards // 2) : (group + 1) * (shards // 2), k * own : (k + 1) * own, lanes]
        return block.reshape(lanes_half, -1)

    for group in range(2):
        total = contract(shifted[0], taps_of(0, group), ((1,), (1,)))
        for k in range(1, 5):
            total = total + contract(shifted[k], taps_of(k, group), ((1,), (1,)))
        conv[:, group * lanes_half : (group + 1) * lanes_half] = total

    def section_rows(at):
        here = pl.ds(at, step_rows)
        c = conv[here, :]
        value = x_ref[here, :].astype(F32) + c * jax.nn.sigmoid(c)
        for j in range(chans // 128):
            section[j, here, :] = value[:, j * 128 : (j + 1) * 128]

    chunks(section_rows)
    pool_rows = 16

    def pool(i):
        at = i * pool_rows
        here = slice(at, at + pool_rows)
        even, odd = (
            jnp.concatenate(
                [section[j, pl.ds(2 * at + i, pool_rows, stride=2), :] for j in range(chans // 128)], axis=1
            )
            for i in range(2)
        )
        squares = jnp.sum(even * even, axis=-1, keepdims=True) + jnp.sum(odd * odd, axis=-1, keepdims=True)
        r = lax.rsqrt(squares / width + EPS)
        rtwo[here, :] = jnp.broadcast_to(r, (pool_rows, 128))
        for j, value in enumerate((even * r, odd * r)):
            lanes = slice(j * chans, (j + 1) * chans)
            atwo[here, lanes] = value
            all_mid[p.seq, here, lanes] = (value * gain_mid_ref[j : j + 1, :]).astype(BF16)

    for i in range(half // pool_rows):
        pool(i)
    mid.start(all_mid.at[p.seq])

    mid_in(0)
    mid_in(1)
    g_own[...] = jnp.zeros_like(g_own)

    def pool_back(i):
        at = i * pool_rows
        here = slice(at, at + pool_rows)
        r = rtwo[here, 0:1]
        grads, terms = [], 0.0
        for j in range(2):
            lanes = slice(j * chans, (j + 1) * chans)
            there = pl.ds(pl.multiple_of(p.z * half + at, 16), pool_rows)
            grad = sums[3, there, lanes]
            for d in range(3):
                grad = grad + z_recv[d, here, lanes].astype(F32)
            a = atwo[here, lanes]
            g_own[1 + j : 2 + j, :] += jnp.sum(grad * a, axis=0, keepdims=True)
            g = gain_mid_ref[j : j + 1, :] * grad
            terms = terms + jnp.sum(g * a, axis=-1, keepdims=True)
            grads.append((g, a))
        for j, (g, a) in enumerate(grads):
            value = r * (g - a * (terms / width))
            for n in range(chans // 128):
                section_grad[n, pl.ds(2 * at + j, pool_rows, stride=2), :] = value[:, n * 128 : (n + 1) * 128]

    def section_grad_rows(here):
        return jnp.concatenate([section_grad[n, here, :] for n in range(chans // 128)], axis=1)

    for i in range(half // pool_rows):
        pool_back(i)

    def conv_back(at):
        here = pl.ds(at, step_rows)
        c = conv[here, :]
        s = jax.nn.sigmoid(c)
        grad = section_grad_rows(here) * s * (1.0 + c * (1.0 - s))
        ext_back[pl.ds(8 + at, step_rows), :] = grad.astype(BF16).astype(F32)

    chunks(conv_back)
    wire.send("tail back", ext_back.at[pl.ds(length, 8)], halo.at[2], seq_peer(1))
    wire.send("head back", ext_back.at[pl.ds(8, 8)], halo.at[3], seq_peer(nlast))
    for j in range(chans // 128):
        lanes = slice(j * 128, (j + 1) * 128)
        cols[lanes, :] = ext_back[8 : 8 + length, lanes].T.astype(BF16)

    for z in range(4):
        for y in range(4):
            block = 4 * y + z
            cols_by_z[z, y * own : (y + 1) * own, :] = cols[block * own : (block + 1) * own, :]
    for d in (1, 3, 2):
        wire.send(("cols", d), cols_by_z.at[wrap4(p.z + d)], all_cols.at[p.z], p.z_peer(d))
    all_cols[p.z] = cols_by_z[p.z]
    mid.own(1)
    mid.near(0)

    wire.recv("tail back", halo.at[2])
    wire.recv("head back", halo.at[3])
    edges(ext_back, halo.at[pl.ds(2, 2)])
    for k in range(5):
        shifted[k] = ext_back[10 - k : 10 - k + length, :].astype(BF16)

    def through(n):
        lanes = slice(n * lanes_half, (n + 1) * lanes_half)
        total = None
        for k in range(5):
            for group in range(2):
                left = shifted[k, :, group * lanes_half : (group + 1) * lanes_half]
                term = contract(left, taps_of(k, group, lanes), ((1,), (0,)))
                total = term if total is None else total + term
        normed_grad[:, lanes] = total

    def project(step, last=False):
        block = all_mid[pl.ds(wrap4(p.y + step) * 4, 4)].reshape(span_rows, width)
        qkv_ref[:, column_lanes(step)] = contract(wt_ref[...], block, ((1,), (1,))).astype(BF16)
        left = cot_ref[:, column_lanes(step)]
        for n in range(width // tile):
            span = slice(n * tile, (n + 1) * tile)
            term = contract(left, all_mid[pl.ds(wrap4(p.y + step) * 4, 4), :, span].reshape(span_rows, tile), ((1,), (0,)))
            if step != 0:
                term = term + pacc[:, span]
            if last:
                high = term.shape[0]
                for j in range(tile // 128):
                    at = (n * (tile // 128) + j) * high
                    p_packed[at : at + high, :] = term[:, j * 128 : (j + 1) * 128].astype(BF16)
            else:
                pacc[:, span] = term

    through(0)
    mid.own(3)
    mid.near(1)
    through(1)

    def last_rows(at):
        here = pl.ds(at, step_rows)
        _, r, a = first_norm(at)
        grad = normed_grad[here, :]
        h = gain_in_ref[...] * grad
        g_own[0:1, :] += jnp.sum(grad * a, axis=0, keepdims=True)
        mean = jnp.mean(h * a, axis=-1, keepdims=True)
        input_grad_ref[here, :] = (section_grad_rows(here) + r * (h - a * mean)).astype(BF16)

    chunks(last_rows)
    gains = GainSum(wire, p, g_core, g_held, g_got)
    gains.start(g_own)

    mid.own(2)
    mid.near(3)

    for d in (1, 3, 2):
        wire.recv(("rows", d), line_rows.at[wrap4(p.z - d)])

    @pl.loop(0, 4)
    def _(z):
        slab[...] = line_rows[z].astype(F32)
        for k in range(5):
            at = pl.ds(pl.multiple_of(z * length, 128), length)
            line_shifted[k, at, :] = slab[6 + k : 6 + k + length, :].astype(BF16)

    for d in (1, 3, 2):
        wire.recv(("cols", d), all_cols.at[wrap4(p.z - d)])
    left = jnp.concatenate([all_cols[z] for z in range(4)], axis=1)
    high = 5 * own
    for k in range(5):
        for n in range(chans // tile):
            term = contract(left, line_shifted[k, :, n * tile : (n + 1) * tile], ((1,), (0,)))
            for j in range(tile // 128):
                at = (n * (tile // 128) + j) * high + k * own
                for y in range(4):
                    value = term[y * own : (y + 1) * own, j * 128 : (j + 1) * 128]
                    k_packed[y, at : at + own, :] = value.astype(BF16)

    def zero_rest(packed, used):
        packed[used:, :] = jnp.zeros((packed.shape[0] - used, 128), BF16)

    for y in range(4):
        zero_rest(k_packed.at[y], high * (chans // 128))
    zero_rest(p_packed, wt_ref.shape[0] * (width // 128))
    kernel_sum = ReduceOverY(wire, p, "k", k_z.shape[1], scale, k_packed, k_core, k_csum, k_x, k_xsum, k_z, k_out)
    proj_sum = Reduce(wire, p, "p", p_z.shape[1], scale, p_packed, p_core, p_csum, p_x, p_xsum, p_z, p_out)
    kernel_sum.core()
    mid.near(2)
    gains.first(g_own)
    kernel_sum.y(k_ysum, k_y)
    project(0)
    project(1)
    project(-1)
    gains.onward(1)
    for d in mid.order:
        mid.far(d)
    project(2, last=True)
    proj_sum.core()
    kernel_sum.x()
    gains.onward(2)
    proj_sum.x()
    kernel_sum.z()
    gains.onward(3)
    proj_sum.z()
    kernel_sum.zz()
    gains_ref[...] = gains.total(3) * scale
    proj_sum.zz()
    kernel_sum.xx()
    proj_sum.xx()
    kernel_sum.cc()
    proj_sum.cc()
    kernel_sum.end()
    for j in range(chans // 128):
        kernel_ref[:, j * 128 : (j + 1) * 128] = k_out[j * high : (j + 1) * high, :]
    proj_sum.end()
    high = wt_ref.shape[0]
    for j in range(width // 128):
        proj_ref[:, j * 128 : (j + 1) * 128] = p_out[j * high : (j + 1) * high, :]
    wire.drain()


def reduce_scratch(elements, over_y=0):
    rows = -(-elements // (128 * 32 * 16)) * 16
    lead = (over_y,) if over_y else ()
    shapes = [lead + (32 * rows, 128), lead + (16 * rows, 128), (16 * rows, 128)]
    shapes += [(3, 4 * rows, 128), (4 * rows, 128), (3, rows, 128), (32 * rows, 128)]
    if over_y:
        shapes += [(over_y, 16 * rows, 128), (over_y - 1, 16 * rows, 128)]
    return [pltpu.VMEM(shape, BF16) for shape in shapes]


def body(section_input, conv_kernel, qkv_weight, gain_in, gain_mid, qkv_cotangent):
    x = section_input[0]
    length, chans = x.shape
    half = length // 2
    width = 2 * chans
    shards = lax.axis_size("seq")
    own = conv_kernel.shape[2]
    high = qkv_weight.shape[1]
    scale = 1.0 / math.sqrt(lax.axis_size("dp") * shards * half)
    taps = jnp.transpose(conv_kernel, (0, 2, 1)).reshape(5 * own, chans)
    taps = jnp.pad(taps, ((0, -(5 * own) % 64), (0, 0)))
    positions = shards * half
    column = positions // 4
    vmem = pl.BlockSpec(memory_space=pltpu.VMEM)
    gain_shape = (8, chans)
    copies = 144
    qkv, input_grad, kernel, proj, gains = pl.pallas_call(
        functools.partial(whole_kernel, scale, own),
        name="whole",
        out_shape=(
            jax.ShapeDtypeStruct((high, positions), BF16),
            jax.ShapeDtypeStruct((length, chans), BF16),
            jax.ShapeDtypeStruct((5 * own, chans), BF16),
            jax.ShapeDtypeStruct((high, width), BF16),
            jax.ShapeDtypeStruct(gain_shape, F32),
        ),
        in_specs=[vmem] * 6,
        out_specs=(vmem,) * 5,
        scratch_shapes=[
            pltpu.VMEM((4, length + 16, chans), BF16),
            pltpu.VMEM((5, 4 * length, chans), BF16),
            pltpu.VMEM((shards,) + taps.shape, BF16),
            pltpu.VMEM((shards, half, width), BF16),
            pltpu.VMEM((4, 4 * own, length), BF16),
            pltpu.VMEM((length + 16, chans), F32),
            pltpu.VMEM((length + 16, chans), F32),
            pltpu.VMEM((length + 16, chans), F32),
            pltpu.VMEM((4, 8, chans), F32),
            pltpu.VMEM((5, length, chans), BF16),
            pltpu.VMEM((length, chans), F32),
            pltpu.VMEM((chans // 128, length, 128), F32),
            pltpu.VMEM((half, width), F32),
            pltpu.VMEM((half, 128), F32),
            pltpu.VMEM((chans // 128, length, 128), F32),
            pltpu.VMEM((length, chans), F32),
            pltpu.VMEM((chans, length), BF16),
            pltpu.VMEM((4, 4 * own, length), BF16),
            pltpu.VMEM((4, column, high), BF16),
            pltpu.VMEM((4, column, width), F32),
            pltpu.VMEM((column, width), BF16),
            pltpu.VMEM((2, column // 2, width), BF16),
            pltpu.VMEM((2, column, width), BF16),
            pltpu.VMEM((2, column, width), BF16),
            pltpu.VMEM((4, half, width), BF16),
            pltpu.VMEM((3, half, width), BF16),
            pltpu.VMEM((high, width), F32),
            *reduce_scratch(5 * own * chans, 4),
            *reduce_scratch(high * width),
            pltpu.VMEM(gain_shape, F32),
            pltpu.VMEM(gain_shape, F32),
            pltpu.VMEM((4,) + gain_shape, F32),
            pltpu.VMEM((4, 3) + gain_shape, F32),
            pltpu.SemaphoreType.DMA((copies,)),
            pltpu.SemaphoreType.DMA((copies,)),
            pltpu.SemaphoreType.DMA((1,)),
        ],
        compiler_params=pltpu.CompilerParams(collective_id=0, has_side_effects=True, vmem_limit_bytes=60 << 20),
    )(x, taps, qkv_weight.T, qkv_cotangent[0].T, gain_in[None], gain_mid.reshape(2, chans))
    return (
        qkv.T[None],
        input_grad[None],
        jnp.transpose(kernel.reshape(5, own, chans), (0, 2, 1)),
        gains[0],
        gains[1:3].reshape(width),
        proj.T,
    )


def solution(mesh):
    placed = (
        P("dp", "seq", None),
        P(None, None, "seq"),
        P(None, "seq"),
        P(),
        P(),
        P("dp", None, "seq"),
    )
    return jax.shard_map(
        body,
        mesh=mesh,
        in_specs=placed,
        out_specs=(
            P("dp", None, "seq"),
            P("dp", "seq", None),
            P(None, None, "seq"),
            P(),
            P(),
            P(None, "seq"),
        ),
        check_vma=False,
    )
```

```python
import functools
import math

import jax
import jax.numpy as jnp
from jax import lax
from jax.experimental import pallas as pl
from jax.experimental.pallas import tpu as pltpu
from jax.sharding import PartitionSpec as P

EPS = 1e-06
MESH = pl.DeviceIdType.MESH
F32 = jnp.float32
BF16 = jnp.bfloat16


def wrap4(i):
    return lax.rem(i + 8, 4)


class Place:
    def __init__(self):
        self.dp = lax.axis_index("dp")
        self.seq = lax.axis_index("seq")
        self.z_hi = self.dp // 8
        self.x = lax.rem(self.dp // 2, 4)
        self.core = lax.rem(self.dp, 2)
        self.y = self.seq // 4
        self.z = lax.rem(self.seq, 4)

    def at_seq(self, y, z):
        return (self.dp, y * 4 + z)

    def y_peer(self, step):
        return self.at_seq(wrap4(self.y + step), self.z)

    def z_peer(self, step):
        return self.at_seq(self.y, wrap4(self.z + step))

    def x_peer(self, step):
        return (self.z_hi * 8 + wrap4(self.x + step) * 2 + self.core, self.seq)

    def z_hi_peer(self, step):
        return (wrap4(self.z_hi + step) * 8 + self.x * 2 + self.core, self.seq)

    def other_core(self):
        return (self.z_hi * 8 + self.x * 2 + 1 - self.core, self.seq)


class Wire:
    def __init__(self, send_sems, recv_sems, anyone):
        self.send_sems = send_sems
        self.recv_sems = recv_sems
        self.anyone = anyone
        self.started = []
        self.names = {}

    def number(self, name):
        return self.names.setdefault(name, len(self.names))

    def send(self, name, src, dst, device):
        k = self.number(name)
        copy = pltpu.make_async_remote_copy(
            src_ref=src,
            dst_ref=dst,
            send_sem=self.send_sems.at[k],
            recv_sem=self.recv_sems.at[k],
            device_id=device,
            device_id_type=MESH,
        )
        copy.start()
        self.started.append(copy)

    def recv(self, name, ref):
        k = self.number(name)
        pltpu.make_async_remote_copy(
            src_ref=ref,
            dst_ref=ref,
            send_sem=self.send_sems.at[k],
            recv_sem=self.recv_sems.at[k],
            device_id=self.anyone,
            device_id_type=MESH,
        ).wait_recv()

    def drain(self):
        for copy in self.started:
            copy.wait_send()


class Gather:
    order = (0, 1, 3, 2)

    def __init__(self, wire, place, tag, view):
        self.wire, self.place, self.tag, self.view = wire, place, tag, view

    def block(self, step, d):
        p = self.place
        return self.view(wrap4(p.y + step) * 4 + wrap4(p.z - d))

    def round_ring(self, d, src):
        for step in (1, -1):
            self.wire.send((self.tag, "y", step, d), src, self.block(0, d), self.place.y_peer(step))

    def start(self, src):
        for d in (1, 3, 2):
            self.wire.send((self.tag, "z", d), src, self.block(0, 0), self.place.z_peer(d))
        self.round_ring(0, src)

    def own(self, d):
        got = self.block(0, d)
        self.wire.recv((self.tag, "z", d), got)
        self.round_ring(d, got)

    def near(self, d):
        for step in (1, -1):
            got = self.block(-step, d)
            self.wire.recv((self.tag, "y", step, d), got)
            if (step == 1) == (d in (0, 1)):
                self.wire.send((self.tag, "relay", d), got, got, self.place.y_peer(step))

    def far(self, d):
        self.wire.recv((self.tag, "relay", d), self.block(2, d))


class Reduce:
    ways = (1, 3, 2)

    def __init__(self, wire, place, tag, rows, scale, packed, core_recv, core_sum, x_recv, x_sum, z_recv, out):
        self.wire, self.place, self.tag, self.rows, self.scale = wire, place, tag, rows, scale
        self.packed, self.core_recv, self.core_sum = packed, core_recv, core_sum
        self.x_recv, self.x_sum, self.z_recv, self.out = x_recv, x_sum, z_recv, out

    def span(self, blocks, count):
        return pl.ds(pl.multiple_of(blocks * self.rows, 16), count * self.rows)

    def core(self):
        p = self.place
        self.wire.send((self.tag, "core"), self.packed.at[self.span((1 - p.core) * 16, 16)], self.core_recv, p.other_core())

    def before_x(self):
        self.wire.recv((self.tag, "core"), self.core_recv)

    def chip_total(self, x):
        mine = self.packed[self.span(self.place.core * 16 + x * 4, 4), :].astype(F32)
        return mine + self.core_recv[self.span(x * 4, 4), :].astype(F32)

    def x(self):
        p = self.place
        self.before_x()

        def add(x):
            self.core_sum[self.span(x * 4, 4), :] = self.chip_total(x).astype(BF16)

        for d in self.ways:
            to = wrap4(p.x + d)
            add(to)
            self.wire.send((self.tag, "x", d), self.core_sum.at[self.span(to * 4, 4)], self.x_recv.at[d - 1], p.x_peer(d))
        add(p.x)

    def z(self):
        p = self.place
        for d in self.ways:
            self.wire.recv((self.tag, "x", d), self.x_recv.at[d - 1])

        def add(z):
            total = self.core_sum[self.span(p.x * 4 + z, 1), :].astype(F32)
            here = self.span(z, 1)
            for d in self.ways:
                total = total + self.x_recv[d - 1, here, :].astype(F32)
            self.x_sum[here, :] = total.astype(BF16)

        for d in (2, 1, 3):
            to = wrap4(p.z_hi + d)
            add(to)
            self.wire.send((self.tag, "z", d), self.x_sum.at[self.span(to, 1)], self.z_recv.at[d - 1], p.z_hi_peer(d))
        add(p.z_hi)

    def zz(self):
        p = self.place
        total = self.x_sum[self.span(p.z_hi, 1), :].astype(F32)
        for d in self.ways:
            self.wire.recv((self.tag, "z", d), self.z_recv.at[d - 1])
            total = total + self.z_recv[d - 1].astype(F32)
        here = self.span(p.core * 16 + p.x * 4 + p.z_hi, 1)
        self.out[here, :] = (total * self.scale).astype(BF16)
        mine = self.out.at[here]
        for d in (2, 1, 3):
            self.wire.send((self.tag, "zz", d), mine, mine, p.z_hi_peer(d))
        self.to_x(0)

    def final(self, core, dx, dz, count=1):
        p = self.place
        z = wrap4(p.z_hi - dz) if count == 1 else 0
        return self.out.at[self.span(core * 16 + wrap4(p.x - dx) * 4 + z, count)]

    def to_x(self, dz):
        p = self.place
        mine = self.final(p.core, 0, dz)
        for d in self.ways:
            self.wire.send((self.tag, "xx", d, dz), mine, mine, p.x_peer(d))

    def to_core(self, dx):
        mine = self.final(self.place.core, dx, 0, 4)
        self.wire.send((self.tag, "cc", dx), mine, mine, self.place.other_core())

    def xx(self):
        for dz in (1, 3, 2):
            self.wire.recv((self.tag, "zz", dz), self.final(self.place.core, 0, dz))
            self.to_x(dz)
        self.to_core(0)

    def cc(self):
        for dx in self.ways:
            for dz in (0, 1, 3, 2):
                self.wire.recv((self.tag, "xx", dx, dz), self.final(self.place.core, dx, dz))
            self.to_core(dx)

    def end(self):
        for dx in (0, 1, 3, 2):
            self.wire.recv((self.tag, "cc", dx), self.final(1 - self.place.core, dx, 0, 4))


class ReduceOverY(Reduce):
    def core(self):
        p = self.place
        theirs = self.packed.at[:, self.span((1 - p.core) * 16, 16)]
        self.wire.send((self.tag, "core"), theirs, self.core_recv, p.other_core())

    def y(self, sums, got):
        p = self.place
        self.y_sums, self.y_got = sums, got
        self.wire.recv((self.tag, "core"), self.core_recv)

        def add(y):
            mine = self.packed[y, self.span(p.core * 16, 16), :].astype(F32)
            sums[y] = (mine + self.core_recv[y].astype(F32)).astype(BF16)

        for d in self.ways:
            to = wrap4(p.y + d)
            add(to)
            self.wire.send((self.tag, "y", d), sums.at[to], got.at[d - 1], p.y_peer(d))
        add(p.y)

    def before_x(self):
        for d in self.ways:
            self.wire.recv((self.tag, "y", d), self.y_got.at[d - 1])

    def chip_total(self, x):
        here = self.span(x * 4, 4)
        total = self.y_sums[self.place.y, here, :].astype(F32)
        for d in range(3):
            total = total + self.y_got[d, here, :].astype(F32)
        return total


class GainSum:
    ways = (1, 3, 2)

    def __init__(self, wire, place, core_recv, held, got):
        self.wire, self.core_recv, self.held, self.got = wire, core_recv, held, got
        self.place = place
        self.peers = (place.x_peer, place.z_hi_peer, place.z_peer, place.y_peer)

    def start(self, src):
        self.wire.send("gain", src, self.core_recv, self.place.other_core())

    def spread(self, stage):
        for d in self.ways:
            self.wire.send(("gain", stage, d), self.held.at[stage], self.got.at[stage, d - 1], self.peers[stage](d))

    def total(self, stage):
        value = self.held[stage]
        for d in self.ways:
            self.wire.recv(("gain", stage, d), self.got.at[stage, d - 1])
            value = value + self.got[stage, d - 1]
        return value

    def first(self, src):
        self.wire.recv("gain", self.core_recv)
        self.held[0] = src[...] + self.core_recv[...]
        self.spread(0)

    def onward(self, stage):
        self.held[stage] = self.total(stage - 1)
        self.spread(stage)


def contract(a, b, dims):
    return lax.dot_general(a, b, (dims, ((), ())), preferred_element_type=F32)


def whole_kernel(
    scale, own, x_ref, taps_ref, wt_ref, cot_ref, gain_ref,
    qkv_ref, input_grad_ref, kernel_ref, proj_ref, gain_in_out, gain_mid_out,
    line_rows, line_shifted, all_taps, all_mid, all_cols, slab,
    ext, ext_back, halo, shifted, conv, section, atwo, rtwo, section_grad, normed_grad, cols, cols_by_z,
    part, sums, far_send, far_recv, near_send, near_recv, column_send, z_recv,
    pacc,
    k_packed, k_core, k_csum, k_x, k_xsum, k_z, k_out, k_ysum, k_y,
    p_packed, p_core, p_csum, p_x, p_xsum, p_z, p_out,
    g_own, g_core, g_held, g_got,
    send_sems, recv_sems,
):
    p = Place()
    wire = Wire(send_sems, recv_sems, p.other_core())
    length, chans = x_ref.shape
    half = length // 2
    width = 2 * chans
    shards = all_mid.shape[0]
    nlast = shards - 1

    def seq_peer(d):
        return (p.dp, lax.rem(p.seq + d, shards))

    peers = [seq_peer(1), seq_peer(nlast), p.other_core()]
    peers += [peer(d) for peer in (p.x_peer, p.y_peer, p.z_peer, p.z_hi_peer) for d in (1, 2, 3)]
    own_rows, pad_rows = taps_ref.shape[0], all_taps.shape[1]
    all_taps[p.seq, 0:own_rows, :] = taps_ref[...]
    all_taps[p.seq, own_rows:pad_rows, :] = jnp.zeros((pad_rows - own_rows, chans), BF16)
    barrier = pltpu.get_barrier_semaphore()
    for peer in peers:
        pl.semaphore_signal(barrier, inc=1, device_id=peer, device_id_type=MESH)

    step_rows = 32

    def chunks(body, count=length, size=step_rows):
        @pl.loop(0, count // size)
        def _(i):
            body(pl.multiple_of(i * size, size))

    def first_norm(at, size=step_rows):
        x = x_ref[pl.ds(at, size), :].astype(F32)
        r = lax.rsqrt(jnp.mean(x * x, axis=-1, keepdims=True) + EPS)
        return x, r, x * r

    def norm_rows(at):
        normed = (first_norm(at)[2] * gain_ref[0:1, :]).astype(BF16)
        ext[pl.ds(8 + at, step_rows), :] = normed.astype(F32)

    chunks(norm_rows)
    pl.semaphore_wait(barrier, len(peers))

    lanes_half = chans // 2
    whole_rows = pad_rows // 4
    quarter = (pad_rows - whole_rows) // 4

    def core_lanes(core):
        return pl.ds(pl.multiple_of(core * lanes_half, 128), lanes_half)

    def piece(x):
        return pl.ds(pl.multiple_of(whole_rows + x * quarter, 16), quarter)

    my_lanes = core_lanes(p.core)
    taps_part = Gather(wire, p, "part", lambda block: all_taps.at[block, piece(p.x), my_lanes])
    taps_whole = Gather(wire, p, "whole", lambda block: all_taps.at[block, pl.ds(0, whole_rows), my_lanes])
    mid = Gather(wire, p, "mid", lambda block: all_mid.at[block])
    for taps in (taps_part, taps_whole):
        taps.start(taps.block(0, 0))
    wire.send("tail", ext.at[pl.ds(length, 8)], halo.at[0], seq_peer(1))
    wire.send("head", ext.at[pl.ds(8, 8)], halo.at[1], seq_peer(nlast))

    def x_part(x, column):
        return all_taps.at[pl.ds(wrap4(p.y + column) * 4, 4), piece(x), my_lanes]

    def x_send(column):
        mine = x_part(p.x, column)
        for way in (1, -1):
            wire.send(("x", way, column), mine, mine, p.x_peer(way))

    def x_relay(column):
        for way in (1, -1):
            got = x_part(wrap4(p.x - way), column)
            wire.recv(("x", way, column), got)
            if (way == 1) == (column in (0, 1)):
                wire.send(("xx", column), got, got, p.x_peer(way))

    def core_part(core, column):
        return all_taps.at[pl.ds(wrap4(p.y + column) * 4, 4), :, core_lanes(core)]

    def core_send(column):
        wire.recv(("xx", column), x_part(wrap4(p.x + 2), column))
        mine = core_part(p.core, column)
        wire.send(("core", column), mine, mine, p.other_core())

    span_rows = cot_ref.shape[1] // 4
    span_half = span_rows // 2
    tile = 256
    slot_of = {2: 0, 1: 1, -1: 2, 0: 3}

    def column_lanes(step):
        return pl.ds(pl.multiple_of(wrap4(p.y + step) * span_rows, 128), span_rows)

    def half_lanes(h):
        return pl.ds(h * chans, chans)

    def product(step, h):
        if h == 0:
            part[slot_of[step]] = cot_ref[:, column_lanes(step)].T

        @pl.loop(0, chans // tile)
        def _(n):
            span = pl.ds(pl.multiple_of(h * chans + n * tile, tile), tile)
            sums[slot_of[step], :, span] = contract(part[slot_of[step]], wt_ref[:, span], ((1,), (0,)))

    def far_out(h):
        lanes = half_lanes(h)
        far_send[:, lanes] = sums[0, :, lanes].astype(BF16)
        wire.send(("far+", h), far_send.at[pl.ds(0, span_half), lanes], far_recv.at[0, :, lanes], p.y_peer(1))
        wire.send(("far-", h), far_send.at[pl.ds(span_half, span_half), lanes], far_recv.at[1, :, lanes], p.y_peer(-1))

    def near_out(h):
        lanes = half_lanes(h)
        wire.recv(("far+", h), far_recv.at[0, :, lanes])
        near_send[0, :span_half, lanes] = (sums[1, :span_half, lanes] + far_recv[0, :, lanes].astype(F32)).astype(BF16)
        near_send[0, span_half:, lanes] = sums[1, span_half:, lanes].astype(BF16)
        wire.send(("near+", h), near_send.at[0, :, lanes], near_recv.at[0, :, lanes], p.y_peer(1))
        wire.recv(("far-", h), far_recv.at[1, :, lanes])
        near_send[1, :span_half, lanes] = sums[2, :span_half, lanes].astype(BF16)
        near_send[1, span_half:, lanes] = (sums[2, span_half:, lanes] + far_recv[1, :, lanes].astype(F32)).astype(BF16)
        wire.send(("near-", h), near_send.at[1, :, lanes], near_recv.at[1, :, lanes], p.y_peer(-1))

    def mid_out(h):
        lanes = half_lanes(h)
        wire.recv(("near+", h), near_recv.at[0, :, lanes])
        wire.recv(("near-", h), near_recv.at[1, :, lanes])

        @pl.loop(0, 4)
        def _(i):
            at = pl.ds(pl.multiple_of(i * half, 16), half)
            total = sums[3, at, lanes] + near_recv[0, at, lanes].astype(F32) + near_recv[1, at, lanes].astype(F32)
            sums[3, at, lanes] = total
            column_send[i, :, lanes] = total.astype(BF16)

        for d in (1, 3, 2):
            wire.send(("mid", h, d), column_send.at[wrap4(p.z + d), :, lanes], z_recv.at[d - 1, :, lanes], p.z_peer(d))

    def mid_in(h):
        for d in (1, 3, 2):
            wire.recv(("mid", h, d), z_recv.at[d - 1, :, half_lanes(h)])

    def edges(into, recv):
        into[0:8, :] = jnp.where(p.seq > 0, recv[0], 0.0)
        into[length + 8 : length + 16, :] = jnp.where(p.seq < nlast, recv[1], 0.0)

    product(2, 0)
    far_out(0)
    product(2, 1)
    for d in (1, 3, 2):
        taps_part.own(d)
    x_send(0)
    for d in (1, 3, 2):
        taps_whole.own(d)
    far_out(1)
    wire.recv("tail", halo.at[0])
    wire.recv("head", halo.at[1])
    edges(ext, halo)
    line_rows[p.z] = ext[...].astype(BF16)
    for d in (1, 3, 2):
        wire.send(("rows", d), line_rows.at[p.z], line_rows.at[p.z], p.z_peer(d))
    for d in taps_part.order:
        taps_part.near(d)
    x_send(1)
    x_send(-1)
    for d in taps_whole.order:
        taps_whole.near(d)
    product(1, 0)
    product(-1, 0)
    near_out(0)
    for d in taps_part.order:
        taps_part.far(d)
    x_send(2)
    product(1, 1)
    product(-1, 1)
    near_out(1)
    x_relay(0)
    product(0, 0)
    product(0, 1)
    for d in taps_whole.order:
        taps_whole.far(d)
    for k in range(5):
        shifted[k] = ext[6 + k : 6 + k + length, :].astype(BF16)
    x_relay(1)
    x_relay(-1)
    core_send(0)
    x_relay(2)
    core_send(1)
    core_send(-1)
    core_send(2)
    mid_out(0)
    for column in (0, 1, -1, 2):
        wire.recv(("core", column), core_part(1 - p.core, column))

    def taps_of(k, group, lanes=slice(None)):
        block = all_taps[group * (shards // 2) : (group + 1) * (shards // 2), k * own : (k + 1) * own, lanes]
        return block.reshape(lanes_half, -1)

    for group in range(2):
        total = contract(shifted[0], taps_of(0, group), ((1,), (1,)))
        for k in range(1, 5):
            total = total + contract(shifted[k], taps_of(k, group), ((1,), (1,)))
        conv[:, group * lanes_half : (group + 1) * lanes_half] = total

    def section_rows(at):
        here = pl.ds(at, step_rows)
        c = conv[here, :]
        value = x_ref[here, :].astype(F32) + c * jax.nn.sigmoid(c)
        for j in range(chans // 128):
            section[j, here, :] = value[:, j * 128 : (j + 1) * 128]

    chunks(section_rows)
    pool_rows = 16

    def pool(i):
        at = i * pool_rows
        here = slice(at, at + pool_rows)
        even, odd = (
            jnp.concatenate(
                [section[j, pl.ds(2 * at + i, pool_rows, stride=2), :] for j in range(chans // 128)], axis=1
            )
            for i in range(2)
        )
        squares = jnp.sum(even * even, axis=-1, keepdims=True) + jnp.sum(odd * odd, axis=-1, keepdims=True)
        r = lax.rsqrt(squares / width + EPS)
        rtwo[here, :] = jnp.broadcast_to(r, (pool_rows, 128))
        for j, value in enumerate((even * r, odd * r)):
            lanes = slice(j * chans, (j + 1) * chans)
            atwo[here, lanes] = value
            all_mid[p.seq, here, lanes] = (value * gain_ref[1 + j : 2 + j, :]).astype(BF16)

    for i in range(half // pool_rows):
        pool(i)
    mid.start(all_mid.at[p.seq])
    mid.own(1)
    mid_out(1)
    mid.own(3)
    mid.near(0)
    mid.near(1)
    mid.own(2)

    mid_in(0)
    mid_in(1)
    g_own[...] = jnp.zeros_like(g_own)

    def pool_back(i):
        at = i * pool_rows
        here = slice(at, at + pool_rows)
        r = rtwo[here, 0:1]
        grads, terms = [], 0.0
        for j in range(2):
            lanes = slice(j * chans, (j + 1) * chans)
            there = pl.ds(pl.multiple_of(p.z * half + at, 16), pool_rows)
            grad = sums[3, there, lanes]
            for d in range(3):
                grad = grad + z_recv[d, here, lanes].astype(F32)
            a = atwo[here, lanes]
            g_own[1 + j : 2 + j, :] += jnp.sum(grad * a, axis=0, keepdims=True)
            g = gain_ref[1 + j : 2 + j, :] * grad
            terms = terms + jnp.sum(g * a, axis=-1, keepdims=True)
            grads.append((g, a))
        for j, (g, a) in enumerate(grads):
            value = r * (g - a * (terms / width))
            for n in range(chans // 128):
                section_grad[n, pl.ds(2 * at + j, pool_rows, stride=2), :] = value[:, n * 128 : (n + 1) * 128]

    def section_grad_rows(here):
        return jnp.concatenate([section_grad[n, here, :] for n in range(chans // 128)], axis=1)

    for i in range(half // pool_rows):
        pool_back(i)

    def conv_back(at):
        here = pl.ds(at, step_rows)
        c = conv[here, :]
        s = jax.nn.sigmoid(c)
        grad = section_grad_rows(here) * s * (1.0 + c * (1.0 - s))
        ext_back[pl.ds(8 + at, step_rows), :] = grad.astype(BF16).astype(F32)

    chunks(conv_back)
    wire.send("tail back", ext_back.at[pl.ds(length, 8)], halo.at[2], seq_peer(1))
    wire.send("head back", ext_back.at[pl.ds(8, 8)], halo.at[3], seq_peer(nlast))
    for j in range(chans // 128):
        lanes = slice(j * 128, (j + 1) * 128)
        cols[lanes, :] = ext_back[8 : 8 + length, lanes].T.astype(BF16)

    for z in range(4):
        for y in range(4):
            block = 4 * y + z
            cols_by_z[z, y * own : (y + 1) * own, :] = cols[block * own : (block + 1) * own, :]
    for d in (1, 3, 2):
        wire.send(("cols", d), cols_by_z.at[wrap4(p.z + d)], all_cols.at[p.z], p.z_peer(d))
    all_cols[p.z] = cols_by_z[p.z]
    mid.near(3)

    wire.recv("tail back", halo.at[2])
    wire.recv("head back", halo.at[3])
    edges(ext_back, halo.at[pl.ds(2, 2)])
    for k in range(5):
        shifted[k] = ext_back[10 - k : 10 - k + length, :].astype(BF16)

    def through(n):
        lanes = slice(n * lanes_half, (n + 1) * lanes_half)
        total = None
        for k in range(5):
            for group in range(2):
                left = shifted[k, :, group * lanes_half : (group + 1) * lanes_half]
                term = contract(left, taps_of(k, group, lanes), ((1,), (0,)))
                total = term if total is None else total + term
        normed_grad[:, lanes] = total

    def project(step, last=False):
        block = all_mid[pl.ds(wrap4(p.y + step) * 4, 4)].reshape(span_rows, width)
        qkv_ref[:, column_lanes(step)] = contract(wt_ref[...], block, ((1,), (1,))).astype(BF16)
        left = cot_ref[:, column_lanes(step)]
        for n in range(width // tile):
            span = slice(n * tile, (n + 1) * tile)
            term = contract(left, all_mid[pl.ds(wrap4(p.y + step) * 4, 4), :, span].reshape(span_rows, tile), ((1,), (0,)))
            if step != 0:
                term = term + pacc[:, span]
            if last:
                high = term.shape[0]
                for j in range(tile // 128):
                    at = (n * (tile // 128) + j) * high
                    p_packed[at : at + high, :] = term[:, j * 128 : (j + 1) * 128].astype(BF16)
            else:
                pacc[:, span] = term

    through(0)
    mid.near(2)
    through(1)

    def last_rows(at):
        here = pl.ds(at, step_rows)
        _, r, a = first_norm(at)
        grad = normed_grad[here, :]
        h = gain_ref[0:1, :] * grad
        g_own[0:1, :] += jnp.sum(grad * a, axis=0, keepdims=True)
        mean = jnp.mean(h * a, axis=-1, keepdims=True)
        input_grad_ref[here, :] = (section_grad_rows(here) + r * (h - a * mean)).astype(BF16)

    chunks(last_rows)
    gains = GainSum(wire, p, g_core, g_held, g_got)
    gains.start(g_own)

    for d in (1, 3, 2):
        wire.recv(("rows", d), line_rows.at[wrap4(p.z - d)])

    @pl.loop(0, 4)
    def _(z):
        slab[...] = line_rows[z].astype(F32)
        for k in range(5):
            at = pl.ds(pl.multiple_of(z * length, 128), length)
            line_shifted[k, at, :] = slab[6 + k : 6 + k + length, :].astype(BF16)

    for d in (1, 3, 2):
        wire.recv(("cols", d), all_cols.at[wrap4(p.z - d)])
    left = jnp.concatenate([all_cols[z] for z in range(4)], axis=1)
    high = 5 * own
    for k in range(5):
        for n in range(chans // tile):
            term = contract(left, line_shifted[k, :, n * tile : (n + 1) * tile], ((1,), (0,)))
            for j in range(tile // 128):
                at = (n * (tile // 128) + j) * high + k * own
                for y in range(4):
                    value = term[y * own : (y + 1) * own, j * 128 : (j + 1) * 128]
                    k_packed[y, at : at + own, :] = value.astype(BF16)

    def zero_rest(packed, used):
        packed[used:, :] = jnp.zeros((packed.shape[0] - used, 128), BF16)

    for y in range(4):
        zero_rest(k_packed.at[y], high * (chans // 128))
    zero_rest(p_packed, wt_ref.shape[0] * (width // 128))
    kernel_sum = ReduceOverY(wire, p, "k", k_z.shape[1], scale, k_packed, k_core, k_csum, k_x, k_xsum, k_z, k_out)
    proj_sum = Reduce(wire, p, "p", p_z.shape[1], scale, p_packed, p_core, p_csum, p_x, p_xsum, p_z, p_out)
    kernel_sum.core()
    gains.first(g_own)
    kernel_sum.y(k_ysum, k_y)
    project(0)
    project(1)
    project(-1)
    gains.onward(1)
    for d in mid.order:
        mid.far(d)
    project(2, last=True)
    proj_sum.core()
    kernel_sum.x()
    gains.onward(2)
    proj_sum.x()
    kernel_sum.z()
    gains.onward(3)
    proj_sum.z()
    kernel_sum.zz()
    gain_total = gains.total(3) * scale
    gain_in_out[...] = gain_total[0:1, :]
    gain_mid_out[...] = gain_total[1:3, :]
    proj_sum.zz()
    kernel_sum.xx()
    proj_sum.xx()
    kernel_sum.cc()
    proj_sum.cc()
    kernel_sum.end()
    for j in range(chans // 128):
        kernel_ref[:, j * 128 : (j + 1) * 128] = k_out[j * high : (j + 1) * high, :]
    proj_sum.end()
    high = wt_ref.shape[0]
    for j in range(width // 128):
        proj_ref[:, j * 128 : (j + 1) * 128] = p_out[j * high : (j + 1) * high, :]
    wire.drain()


def reduce_scratch(elements, over_y=0):
    rows = -(-elements // (128 * 32 * 16)) * 16
    lead = (over_y,) if over_y else ()
    shapes = [lead + (32 * rows, 128), lead + (16 * rows, 128), (16 * rows, 128)]
    shapes += [(3, 4 * rows, 128), (4 * rows, 128), (3, rows, 128), (32 * rows, 128)]
    if over_y:
        shapes += [(over_y, 16 * rows, 128), (over_y - 1, 16 * rows, 128)]
    return [pltpu.VMEM(shape, BF16) for shape in shapes]


def body(section_input, conv_kernel, qkv_weight, gain_in, gain_mid, qkv_cotangent):
    x = section_input[0]
    length, chans = x.shape
    half = length // 2
    width = 2 * chans
    shards = lax.axis_size("seq")
    own = conv_kernel.shape[2]
    high = qkv_weight.shape[1]
    scale = 1.0 / math.sqrt(lax.axis_size("dp") * shards * half)
    taps = jnp.transpose(conv_kernel, (0, 2, 1)).reshape(5 * own, chans)
    pad_rows = -(-5 * own // 256) * 256
    positions = shards * half
    column = positions // 4
    vmem = pl.BlockSpec(memory_space=pltpu.VMEM)
    gain_shape = (8, chans)
    copies = 160
    qkv, input_grad, kernel, proj, gain_in_grad, gain_mid_grad = pl.pallas_call(
        functools.partial(whole_kernel, scale, own),
        name="whole",
        out_shape=(
            jax.ShapeDtypeStruct((high, positions), BF16),
            jax.ShapeDtypeStruct((length, chans), BF16),
            jax.ShapeDtypeStruct((5 * own, chans), BF16),
            jax.ShapeDtypeStruct((high, width), BF16),
            jax.ShapeDtypeStruct((1, chans), F32),
            jax.ShapeDtypeStruct((2, chans), F32),
        ),
        in_specs=[vmem] * 5,
        out_specs=(vmem,) * 6,
        scratch_shapes=[
            pltpu.VMEM((4, length + 16, chans), BF16),
            pltpu.VMEM((5, 4 * length, chans), BF16),
            pltpu.VMEM((shards, pad_rows, chans), BF16),
            pltpu.VMEM((shards, half, width), BF16),
            pltpu.VMEM((4, 4 * own, length), BF16),
            pltpu.VMEM((length + 16, chans), F32),
            pltpu.VMEM((length + 16, chans), F32),
            pltpu.VMEM((length + 16, chans), F32),
            pltpu.VMEM((4, 8, chans), F32),
            pltpu.VMEM((5, length, chans), BF16),
            pltpu.VMEM((length, chans), F32),
            pltpu.VMEM((chans // 128, length, 128), F32),
            pltpu.VMEM((half, width), F32),
            pltpu.VMEM((half, 128), F32),
            pltpu.VMEM((chans // 128, length, 128), F32),
            pltpu.VMEM((length, chans), F32),
            pltpu.VMEM((chans, length), BF16),
            pltpu.VMEM((4, 4 * own, length), BF16),
            pltpu.VMEM((4, column, high), BF16),
            pltpu.VMEM((4, column, width), F32),
            pltpu.VMEM((column, width), BF16),
            pltpu.VMEM((2, column // 2, width), BF16),
            pltpu.VMEM((2, column, width), BF16),
            pltpu.VMEM((2, column, width), BF16),
            pltpu.VMEM((4, half, width), BF16),
            pltpu.VMEM((3, half, width), BF16),
            pltpu.VMEM((high, width), F32),
            *reduce_scratch(5 * own * chans, 4),
            *reduce_scratch(high * width),
            pltpu.VMEM(gain_shape, F32),
            pltpu.VMEM(gain_shape, F32),
            pltpu.VMEM((4,) + gain_shape, F32),
            pltpu.VMEM((4, 3) + gain_shape, F32),
            pltpu.SemaphoreType.DMA((copies,)),
            pltpu.SemaphoreType.DMA((copies,)),
        ],
        compiler_params=pltpu.CompilerParams(collective_id=0, has_side_effects=True, vmem_limit_bytes=60 << 20),
    )(x, taps, qkv_weight.T, qkv_cotangent[0].T, jnp.concatenate([gain_in, gain_mid]).reshape(3, chans))
    return (
        qkv.T[None],
        input_grad[None],
        jnp.transpose(kernel.reshape(5, own, chans), (0, 2, 1)),
        gain_in_grad.reshape(chans),
        gain_mid_grad.reshape(width),
        proj.T,
    )


def solution(mesh):
    placed = (
        P("dp", "seq", None),
        P(None, None, "seq"),
        P(None, "seq"),
        P(),
        P(),
        P("dp", None, "seq"),
    )
    return jax.shard_map(
        body,
        mesh=mesh,
        in_specs=placed,
        out_specs=(
            P("dp", None, "seq"),
            P("dp", "seq", None),
            P(None, None, "seq"),
            P(),
            P(),
            P(None, "seq"),
        ),
        check_vma=False,
    )
```

```python
import functools
import math

import jax
import jax.numpy as jnp
from jax import lax
from jax.experimental import pallas as pl
from jax.experimental.pallas import tpu as pltpu
from jax.sharding import PartitionSpec as P

EPS = 1e-06
MESH = pl.DeviceIdType.MESH
F32 = jnp.float32
BF16 = jnp.bfloat16


def wrap4(i):
    return lax.rem(i + 8, 4)


class Place:
    def __init__(self):
        self.dp = lax.axis_index("dp")
        self.seq = lax.axis_index("seq")
        self.z_hi = self.dp // 8
        self.x = lax.rem(self.dp // 2, 4)
        self.core = lax.rem(self.dp, 2)
        self.y = self.seq // 4
        self.z = lax.rem(self.seq, 4)

    def at_seq(self, y, z):
        return (self.dp, y * 4 + z)

    def y_peer(self, step):
        return self.at_seq(wrap4(self.y + step), self.z)

    def z_peer(self, step):
        return self.at_seq(self.y, wrap4(self.z + step))

    def x_peer(self, step):
        return (self.z_hi * 8 + wrap4(self.x + step) * 2 + self.core, self.seq)

    def z_hi_peer(self, step):
        return (wrap4(self.z_hi + step) * 8 + self.x * 2 + self.core, self.seq)

    def other_core(self):
        return (self.z_hi * 8 + self.x * 2 + 1 - self.core, self.seq)


class Wire:
    def __init__(self, send_sems, recv_sems, anyone):
        self.send_sems = send_sems
        self.recv_sems = recv_sems
        self.anyone = anyone
        self.started = []
        self.names = {}

    def number(self, name):
        return self.names.setdefault(name, len(self.names))

    def send(self, name, src, dst, device):
        k = self.number(name)
        copy = pltpu.make_async_remote_copy(
            src_ref=src,
            dst_ref=dst,
            send_sem=self.send_sems.at[k],
            recv_sem=self.recv_sems.at[k],
            device_id=device,
            device_id_type=MESH,
        )
        copy.start()
        self.started.append(copy)

    def recv(self, name, ref):
        k = self.number(name)
        pltpu.make_async_remote_copy(
            src_ref=ref,
            dst_ref=ref,
            send_sem=self.send_sems.at[k],
            recv_sem=self.recv_sems.at[k],
            device_id=self.anyone,
            device_id_type=MESH,
        ).wait_recv()

    def drain(self):
        for copy in self.started:
            copy.wait_send()


class Gather:
    order = (0, 1, 3, 2)

    def __init__(self, wire, place, tag, view):
        self.wire, self.place, self.tag, self.view = wire, place, tag, view

    def block(self, step, d):
        p = self.place
        return self.view(wrap4(p.y + step) * 4 + wrap4(p.z - d))

    def round_ring(self, d, src):
        for step in (1, -1):
            self.wire.send((self.tag, "y", step, d), src, self.block(0, d), self.place.y_peer(step))

    def line(self, ds, src):
        for d in ds:
            self.wire.send((self.tag, "z", d), src, self.block(0, 0), self.place.z_peer(d))

    def start(self, src):
        self.line((1, 3, 2), src)
        self.round_ring(0, src)

    def own(self, d):
        got = self.block(0, d)
        self.wire.recv((self.tag, "z", d), got)
        self.round_ring(d, got)

    def near(self, d):
        for step in (1, -1):
            got = self.block(-step, d)
            self.wire.recv((self.tag, "y", step, d), got)
            if (step == 1) == (d in (0, 1)):
                self.wire.send((self.tag, "relay", d), got, got, self.place.y_peer(step))

    def far(self, d):
        self.wire.recv((self.tag, "relay", d), self.block(2, d))


class Reduce:
    ways = (1, 3, 2)

    def __init__(self, wire, place, tag, rows, scale, packed, core_recv, core_sum, x_recv, x_sum, z_recv, out):
        self.wire, self.place, self.tag, self.rows, self.scale = wire, place, tag, rows, scale
        self.packed, self.core_recv, self.core_sum = packed, core_recv, core_sum
        self.x_recv, self.x_sum, self.z_recv, self.out = x_recv, x_sum, z_recv, out

    def span(self, blocks, count):
        return pl.ds(pl.multiple_of(blocks * self.rows, 16), count * self.rows)

    def core(self):
        p = self.place
        self.wire.send((self.tag, "core"), self.packed.at[self.span((1 - p.core) * 16, 16)], self.core_recv, p.other_core())

    def before_x(self):
        self.wire.recv((self.tag, "core"), self.core_recv)

    def chip_total(self, x):
        mine = self.packed[self.span(self.place.core * 16 + x * 4, 4), :].astype(F32)
        return mine + self.core_recv[self.span(x * 4, 4), :].astype(F32)

    def x(self):
        p = self.place
        self.before_x()

        def add(x):
            self.core_sum[self.span(x * 4, 4), :] = self.chip_total(x).astype(BF16)

        for d in self.ways:
            to = wrap4(p.x + d)
            add(to)
            self.wire.send((self.tag, "x", d), self.core_sum.at[self.span(to * 4, 4)], self.x_recv.at[d - 1], p.x_peer(d))
        add(p.x)

    def z(self):
        p = self.place
        for d in self.ways:
            self.wire.recv((self.tag, "x", d), self.x_recv.at[d - 1])

        def add(z):
            total = self.core_sum[self.span(p.x * 4 + z, 1), :].astype(F32)
            here = self.span(z, 1)
            for d in self.ways:
                total = total + self.x_recv[d - 1, here, :].astype(F32)
            self.x_sum[here, :] = total.astype(BF16)

        for d in (2, 1, 3):
            to = wrap4(p.z_hi + d)
            add(to)
            self.wire.send((self.tag, "z", d), self.x_sum.at[self.span(to, 1)], self.z_recv.at[d - 1], p.z_hi_peer(d))
        add(p.z_hi)

    def zz(self):
        p = self.place
        total = self.x_sum[self.span(p.z_hi, 1), :].astype(F32)
        for d in self.ways:
            self.wire.recv((self.tag, "z", d), self.z_recv.at[d - 1])
            total = total + self.z_recv[d - 1].astype(F32)
        here = self.span(p.core * 16 + p.x * 4 + p.z_hi, 1)
        self.out[here, :] = (total * self.scale).astype(BF16)
        mine = self.out.at[here]
        for d in (2, 1, 3):
            self.wire.send((self.tag, "zz", d), mine, mine, p.z_hi_peer(d))
        self.to_x(0)

    def final(self, core, dx, dz, count=1):
        p = self.place
        z = wrap4(p.z_hi - dz) if count == 1 else 0
        return self.out.at[self.span(core * 16 + wrap4(p.x - dx) * 4 + z, count)]

    def to_x(self, dz):
        p = self.place
        mine = self.final(p.core, 0, dz)
        for d in self.ways:
            self.wire.send((self.tag, "xx", d, dz), mine, mine, p.x_peer(d))

    def to_core(self, dx):
        mine = self.final(self.place.core, dx, 0, 4)
        self.wire.send((self.tag, "cc", dx), mine, mine, self.place.other_core())

    def xx(self):
        for dz in (1, 3, 2):
            self.wire.recv((self.tag, "zz", dz), self.final(self.place.core, 0, dz))
            self.to_x(dz)
        self.to_core(0)

    def cc(self):
        for dx in self.ways:
            for dz in (0, 1, 3, 2):
                self.wire.recv((self.tag, "xx", dx, dz), self.final(self.place.core, dx, dz))
            self.to_core(dx)

    def end(self):
        for dx in (0, 1, 3, 2):
            self.wire.recv((self.tag, "cc", dx), self.final(1 - self.place.core, dx, 0, 4))


class ReduceOverY(Reduce):
    def core(self):
        p = self.place
        theirs = self.packed.at[:, self.span((1 - p.core) * 16, 16)]
        self.wire.send((self.tag, "core"), theirs, self.core_recv, p.other_core())

    def y(self, sums, got):
        p = self.place
        self.y_sums, self.y_got = sums, got
        self.wire.recv((self.tag, "core"), self.core_recv)

        def add(y):
            mine = self.packed[y, self.span(p.core * 16, 16), :].astype(F32)
            sums[y] = (mine + self.core_recv[y].astype(F32)).astype(BF16)

        for d in self.ways:
            to = wrap4(p.y + d)
            add(to)
            self.wire.send((self.tag, "y", d), sums.at[to], got.at[d - 1], p.y_peer(d))
        add(p.y)

    def before_x(self):
        for d in self.ways:
            self.wire.recv((self.tag, "y", d), self.y_got.at[d - 1])

    def chip_total(self, x):
        here = self.span(x * 4, 4)
        total = self.y_sums[self.place.y, here, :].astype(F32)
        for d in range(3):
            total = total + self.y_got[d, here, :].astype(F32)
        return total


class GainSum:
    ways = (1, 3, 2)

    def __init__(self, wire, place, core_recv, held, got):
        self.wire, self.core_recv, self.held, self.got = wire, core_recv, held, got
        self.place = place
        self.peers = (place.x_peer, place.z_hi_peer, place.z_peer, place.y_peer)

    def start(self, src):
        self.wire.send("gain", src, self.core_recv, self.place.other_core())

    def spread(self, stage):
        for d in self.ways:
            self.wire.send(("gain", stage, d), self.held.at[stage], self.got.at[stage, d - 1], self.peers[stage](d))

    def total(self, stage):
        value = self.held[stage]
        for d in self.ways:
            self.wire.recv(("gain", stage, d), self.got.at[stage, d - 1])
            value = value + self.got[stage, d - 1]
        return value

    def first(self, src):
        self.wire.recv("gain", self.core_recv)
        self.held[0] = src[...] + self.core_recv[...]
        self.spread(0)

    def onward(self, stage):
        self.held[stage] = self.total(stage - 1)
        self.spread(stage)


def contract(a, b, dims):
    return lax.dot_general(a, b, (dims, ((), ())), preferred_element_type=F32)


def whole_kernel(
    scale, own, x_ref, taps_ref, wt_ref, cot_ref, gain_ref,
    qkv_ref, input_grad_ref, kernel_ref, proj_ref, gain_in_out, gain_mid_out,
    line_rows, line_shifted, all_taps, all_mid, all_cols, slab,
    ext, ext_back, halo, shifted, conv, section, atwo, rtwo, section_grad, normed_grad, cols, cols_by_z,
    part, sums, far_send, far_recv, near_send, near_recv, column_send, z_recv,
    pacc,
    k_packed, k_core, k_csum, k_x, k_xsum, k_z, k_out, k_ysum, k_y,
    p_packed, p_core, p_csum, p_x, p_xsum, p_z, p_out,
    g_own, g_core, g_held, g_got,
    send_sems, recv_sems,
):
    p = Place()
    wire = Wire(send_sems, recv_sems, p.other_core())
    length, chans = x_ref.shape
    half = length // 2
    width = 2 * chans
    shards = all_mid.shape[0]
    nlast = shards - 1

    def seq_peer(d):
        return (p.dp, lax.rem(p.seq + d, shards))

    peers = [seq_peer(1), seq_peer(nlast), p.other_core()]
    peers += [peer(d) for peer in (p.x_peer, p.y_peer, p.z_peer, p.z_hi_peer) for d in (1, 2, 3)]
    own_rows, pad_rows = taps_ref.shape[0], all_taps.shape[1]
    all_taps[p.seq, 0:own_rows, :] = taps_ref[...]
    all_taps[p.seq, own_rows:pad_rows, :] = jnp.zeros((pad_rows - own_rows, chans), BF16)
    barrier = pltpu.get_barrier_semaphore()
    for peer in peers:
        pl.semaphore_signal(barrier, inc=1, device_id=peer, device_id_type=MESH)

    step_rows = 32

    def chunks(body, count=length, size=step_rows):
        @pl.loop(0, count // size)
        def _(i):
            body(pl.multiple_of(i * size, size))

    def first_norm(at, size=step_rows):
        x = x_ref[pl.ds(at, size), :].astype(F32)
        r = lax.rsqrt(jnp.mean(x * x, axis=-1, keepdims=True) + EPS)
        return x, r, x * r

    def norm_rows(at):
        normed = (first_norm(at)[2] * gain_ref[0:1, :]).astype(BF16)
        ext[pl.ds(8 + at, step_rows), :] = normed.astype(F32)

    chunks(norm_rows)
    pl.semaphore_wait(barrier, len(peers))

    lanes_half = chans // 2
    whole_rows = pad_rows // 4
    quarter = (pad_rows - whole_rows) // 4

    def core_lanes(core):
        return pl.ds(pl.multiple_of(core * lanes_half, 128), lanes_half)

    def piece(x):
        return pl.ds(pl.multiple_of(whole_rows + x * quarter, 16), quarter)

    my_lanes = core_lanes(p.core)
    taps_part = Gather(wire, p, "part", lambda block: all_taps.at[block, piece(p.x), my_lanes])
    taps_whole = Gather(wire, p, "whole", lambda block: all_taps.at[block, pl.ds(0, whole_rows), my_lanes])
    mid_rows = half // 2
    mids = [
        Gather(wire, p, ("mid", i), lambda block, i=i: all_mid.at[block, pl.ds(i * mid_rows, mid_rows)])
        for i in range(2)
    ]
    for taps in (taps_part, taps_whole):
        taps.start(taps.block(0, 0))
    wire.send("tail", ext.at[pl.ds(length, 8)], halo.at[0], seq_peer(1))
    wire.send("head", ext.at[pl.ds(8, 8)], halo.at[1], seq_peer(nlast))

    def x_part(x, column):
        return all_taps.at[pl.ds(wrap4(p.y + column) * 4, 4), piece(x), my_lanes]

    def x_send(column):
        mine = x_part(p.x, column)
        for way in (1, -1):
            wire.send(("x", way, column), mine, mine, p.x_peer(way))

    def x_relay(column):
        for way in (1, -1):
            got = x_part(wrap4(p.x - way), column)
            wire.recv(("x", way, column), got)
            if (way == 1) == (column in (0, 1)):
                wire.send(("xx", column), got, got, p.x_peer(way))

    def core_part(core, column):
        return all_taps.at[pl.ds(wrap4(p.y + column) * 4, 4), :, core_lanes(core)]

    def core_send(column):
        wire.recv(("xx", column), x_part(wrap4(p.x + 2), column))
        mine = core_part(p.core, column)
        wire.send(("core", column), mine, mine, p.other_core())

    span_rows = cot_ref.shape[1] // 4
    span_half = span_rows // 2
    tile = 256
    slot_of = {2: 0, 1: 1, -1: 2, 0: 3}

    def column_lanes(step):
        return pl.ds(pl.multiple_of(wrap4(p.y + step) * span_rows, 128), span_rows)

    def half_lanes(h):
        return pl.ds(h * chans, chans)

    def product(step, h):
        if h == 0:
            part[slot_of[step]] = cot_ref[:, column_lanes(step)].T

        @pl.loop(0, chans // tile)
        def _(n):
            span = pl.ds(pl.multiple_of(h * chans + n * tile, tile), tile)
            sums[slot_of[step], :, span] = contract(part[slot_of[step]], wt_ref[:, span], ((1,), (0,)))

    def far_out(h):
        lanes = half_lanes(h)
        far_send[:, lanes] = sums[0, :, lanes].astype(BF16)
        wire.send(("far+", h), far_send.at[pl.ds(0, span_half), lanes], far_recv.at[0, :, lanes], p.y_peer(1))
        wire.send(("far-", h), far_send.at[pl.ds(span_half, span_half), lanes], far_recv.at[1, :, lanes], p.y_peer(-1))

    def near_out(h):
        lanes = half_lanes(h)
        wire.recv(("far+", h), far_recv.at[0, :, lanes])
        near_send[0, :span_half, lanes] = (sums[1, :span_half, lanes] + far_recv[0, :, lanes].astype(F32)).astype(BF16)
        near_send[0, span_half:, lanes] = sums[1, span_half:, lanes].astype(BF16)
        wire.send(("near+", h), near_send.at[0, :, lanes], near_recv.at[0, :, lanes], p.y_peer(1))
        wire.recv(("far-", h), far_recv.at[1, :, lanes])
        near_send[1, :span_half, lanes] = sums[2, :span_half, lanes].astype(BF16)
        near_send[1, span_half:, lanes] = (sums[2, span_half:, lanes] + far_recv[1, :, lanes].astype(F32)).astype(BF16)
        wire.send(("near-", h), near_send.at[1, :, lanes], near_recv.at[1, :, lanes], p.y_peer(-1))

    def mid_out(h):
        lanes = half_lanes(h)
        wire.recv(("near+", h), near_recv.at[0, :, lanes])
        wire.recv(("near-", h), near_recv.at[1, :, lanes])

        @pl.loop(0, 4)
        def _(i):
            at = pl.ds(pl.multiple_of(i * half, 16), half)
            total = sums[3, at, lanes] + near_recv[0, at, lanes].astype(F32) + near_recv[1, at, lanes].astype(F32)
            sums[3, at, lanes] = total
            column_send[i, :, lanes] = total.astype(BF16)

        for d in (1, 3, 2):
            wire.send(("mid", h, d), column_send.at[wrap4(p.z + d), :, lanes], z_recv.at[d - 1, :, lanes], p.z_peer(d))

    def mid_in(h):
        for d in (1, 3, 2):
            wire.recv(("mid", h, d), z_recv.at[d - 1, :, half_lanes(h)])

    def edges(into, recv):
        into[0:8, :] = jnp.where(p.seq > 0, recv[0], 0.0)
        into[length + 8 : length + 16, :] = jnp.where(p.seq < nlast, recv[1], 0.0)

    product(2, 0)
    far_out(0)
    product(2, 1)
    for d in (1, 3, 2):
        taps_part.own(d)
    x_send(0)
    for d in (1, 3, 2):
        taps_whole.own(d)
    wire.recv("tail", halo.at[0])
    wire.recv("head", halo.at[1])
    edges(ext, halo)
    line_rows[p.z] = ext[...].astype(BF16)
    for d in (1, 3, 2):
        wire.send(("rows", d), line_rows.at[p.z], line_rows.at[p.z], p.z_peer(d))
    for d in taps_part.order:
        taps_part.near(d)
    x_send(1)
    x_send(-1)
    for d in taps_whole.order:
        taps_whole.near(d)
    product(1, 0)
    product(-1, 0)
    near_out(0)
    far_out(1)
    for d in taps_part.order:
        taps_part.far(d)
    x_send(2)
    product(1, 1)
    product(-1, 1)
    x_relay(0)
    product(0, 0)
    product(0, 1)
    for d in taps_whole.order:
        taps_whole.far(d)
    for k in range(5):
        shifted[k] = ext[6 + k : 6 + k + length, :].astype(BF16)
    x_relay(1)
    x_relay(-1)
    x_relay(2)
    core_send(0)
    core_send(1)
    mid_out(0)
    core_send(-1)
    core_send(2)
    near_out(1)
    for column in (0, 1, -1, 2):
        wire.recv(("core", column), core_part(1 - p.core, column))

    def taps_of(k, group, lanes=slice(None)):
        block = all_taps[group * (shards // 2) : (group + 1) * (shards // 2), k * own : (k + 1) * own, lanes]
        return block.reshape(lanes_half, -1)

    for group in range(2):
        total = contract(shifted[0], taps_of(0, group), ((1,), (1,)))
        for k in range(1, 5):
            total = total + contract(shifted[k], taps_of(k, group), ((1,), (1,)))
        conv[:, group * lanes_half : (group + 1) * lanes_half] = total

    def section_rows(at):
        here = pl.ds(at, step_rows)
        c = conv[here, :]
        value = x_ref[here, :].astype(F32) + c * jax.nn.sigmoid(c)
        for j in range(chans // 128):
            section[j, here, :] = value[:, j * 128 : (j + 1) * 128]

    chunks(section_rows)
    pool_rows = 16

    def pool(i):
        at = i * pool_rows
        here = slice(at, at + pool_rows)
        even, odd = (
            jnp.concatenate(
                [section[j, pl.ds(2 * at + i, pool_rows, stride=2), :] for j in range(chans // 128)], axis=1
            )
            for i in range(2)
        )
        squares = jnp.sum(even * even, axis=-1, keepdims=True) + jnp.sum(odd * odd, axis=-1, keepdims=True)
        r = lax.rsqrt(squares / width + EPS)
        rtwo[here, :] = jnp.broadcast_to(r, (pool_rows, 128))
        for j, value in enumerate((even * r, odd * r)):
            lanes = slice(j * chans, (j + 1) * chans)
            atwo[here, lanes] = value
            all_mid[p.seq, here, lanes] = (value * gain_ref[1 + j : 2 + j, :]).astype(BF16)

    for i in range(half // pool_rows):
        pool(i)
    for mid in mids:
        mid.round_ring(0, mid.block(0, 0))
        mid.line((1, 3), mid.block(0, 0))
    mid_out(1)
    for mid in mids:
        mid.line((2,), mid.block(0, 0))
    for d in (1, 3, 2):
        wire.recv(("rows", d), line_rows.at[wrap4(p.z - d)])

    @pl.loop(0, 4)
    def _(z):
        slab[...] = line_rows[z].astype(F32)
        for k in range(5):
            at = pl.ds(pl.multiple_of(z * length, 128), length)
            line_shifted[k, at, :] = slab[6 + k : 6 + k + length, :].astype(BF16)

    for mid in mids:
        mid.own(1)
    for mid in mids:
        mid.own(3)
    for d in (0, 1, 3):
        for mid in mids:
            mid.near(d)

    mid_in(0)
    mid_in(1)
    g_own[...] = jnp.zeros_like(g_own)

    def pool_back(i):
        at = i * pool_rows
        here = slice(at, at + pool_rows)
        r = rtwo[here, 0:1]
        grads, terms = [], 0.0
        for j in range(2):
            lanes = slice(j * chans, (j + 1) * chans)
            there = pl.ds(pl.multiple_of(p.z * half + at, 16), pool_rows)
            grad = sums[3, there, lanes]
            for d in range(3):
                grad = grad + z_recv[d, here, lanes].astype(F32)
            a = atwo[here, lanes]
            g_own[1 + j : 2 + j, :] += jnp.sum(grad * a, axis=0, keepdims=True)
            g = gain_ref[1 + j : 2 + j, :] * grad
            terms = terms + jnp.sum(g * a, axis=-1, keepdims=True)
            grads.append((g, a))
        for j, (g, a) in enumerate(grads):
            value = r * (g - a * (terms / width))
            for n in range(chans // 128):
                section_grad[n, pl.ds(2 * at + j, pool_rows, stride=2), :] = value[:, n * 128 : (n + 1) * 128]

    def section_grad_rows(here):
        return jnp.concatenate([section_grad[n, here, :] for n in range(chans // 128)], axis=1)

    for i in range(half // pool_rows):
        pool_back(i)

    def conv_back(at):
        here = pl.ds(at, step_rows)
        c = conv[here, :]
        s = jax.nn.sigmoid(c)
        grad = section_grad_rows(here) * s * (1.0 + c * (1.0 - s))
        ext_back[pl.ds(8 + at, step_rows), :] = grad.astype(BF16).astype(F32)

    chunks(conv_back)
    wire.send("tail back", ext_back.at[pl.ds(length, 8)], halo.at[2], seq_peer(1))
    wire.send("head back", ext_back.at[pl.ds(8, 8)], halo.at[3], seq_peer(nlast))
    for j in range(chans // 128):
        lanes = slice(j * 128, (j + 1) * 128)
        cols[lanes, :] = ext_back[8 : 8 + length, lanes].T.astype(BF16)

    for z in range(4):
        for y in range(4):
            block = 4 * y + z
            cols_by_z[z, y * own : (y + 1) * own, :] = cols[block * own : (block + 1) * own, :]
    for d in (1, 3, 2):
        wire.send(("cols", d), cols_by_z.at[wrap4(p.z + d)], all_cols.at[p.z], p.z_peer(d))
    all_cols[p.z] = cols_by_z[p.z]
    mids[0].own(2)

    wire.recv("tail back", halo.at[2])
    wire.recv("head back", halo.at[3])
    edges(ext_back, halo.at[pl.ds(2, 2)])
    for k in range(5):
        shifted[k] = ext_back[10 - k : 10 - k + length, :].astype(BF16)

    def through(n):
        lanes = slice(n * lanes_half, (n + 1) * lanes_half)
        total = None
        for k in range(5):
            for group in range(2):
                left = shifted[k, :, group * lanes_half : (group + 1) * lanes_half]
                term = contract(left, taps_of(k, group, lanes), ((1,), (0,)))
                total = term if total is None else total + term
        normed_grad[:, lanes] = total

    def project(step, last=False):
        block = all_mid[pl.ds(wrap4(p.y + step) * 4, 4)].reshape(span_rows, width)
        qkv_ref[:, column_lanes(step)] = contract(wt_ref[...], block, ((1,), (1,))).astype(BF16)
        left = cot_ref[:, column_lanes(step)]
        for n in range(width // tile):
            span = slice(n * tile, (n + 1) * tile)
            term = contract(left, all_mid[pl.ds(wrap4(p.y + step) * 4, 4), :, span].reshape(span_rows, tile), ((1,), (0,)))
            if step != 0:
                term = term + pacc[:, span]
            if last:
                high = term.shape[0]
                for j in range(tile // 128):
                    at = (n * (tile // 128) + j) * high
                    p_packed[at : at + high, :] = term[:, j * 128 : (j + 1) * 128].astype(BF16)
            else:
                pacc[:, span] = term

    through(0)
    mids[1].own(2)
    through(1)

    def last_rows(at):
        here = pl.ds(at, step_rows)
        _, r, a = first_norm(at)
        grad = normed_grad[here, :]
        h = gain_ref[0:1, :] * grad
        g_own[0:1, :] += jnp.sum(grad * a, axis=0, keepdims=True)
        mean = jnp.mean(h * a, axis=-1, keepdims=True)
        input_grad_ref[here, :] = (section_grad_rows(here) + r * (h - a * mean)).astype(BF16)

    chunks(last_rows)
    gains = GainSum(wire, p, g_core, g_held, g_got)
    gains.start(g_own)

    for mid in mids:
        mid.near(2)

    for d in (1, 3, 2):
        wire.recv(("cols", d), all_cols.at[wrap4(p.z - d)])
    left = jnp.concatenate([all_cols[z] for z in range(4)], axis=1)
    high = 5 * own
    for k in range(5):
        for n in range(chans // tile):
            term = contract(left, line_shifted[k, :, n * tile : (n + 1) * tile], ((1,), (0,)))
            for j in range(tile // 128):
                at = (n * (tile // 128) + j) * high + k * own
                for y in range(4):
                    value = term[y * own : (y + 1) * own, j * 128 : (j + 1) * 128]
                    k_packed[y, at : at + own, :] = value.astype(BF16)

    def zero_rest(packed, used):
        packed[used:, :] = jnp.zeros((packed.shape[0] - used, 128), BF16)

    for y in range(4):
        zero_rest(k_packed.at[y], high * (chans // 128))
    zero_rest(p_packed, wt_ref.shape[0] * (width // 128))
    kernel_sum = ReduceOverY(wire, p, "k", k_z.shape[1], scale, k_packed, k_core, k_csum, k_x, k_xsum, k_z, k_out)
    proj_sum = Reduce(wire, p, "p", p_z.shape[1], scale, p_packed, p_core, p_csum, p_x, p_xsum, p_z, p_out)
    kernel_sum.core()
    gains.first(g_own)
    kernel_sum.y(k_ysum, k_y)
    project(0)
    project(1)
    project(-1)
    gains.onward(1)
    for mid in mids:
        for d in mid.order:
            mid.far(d)
    project(2, last=True)
    proj_sum.core()
    kernel_sum.x()
    gains.onward(2)
    proj_sum.x()
    kernel_sum.z()
    gains.onward(3)
    proj_sum.z()
    kernel_sum.zz()
    gain_total = gains.total(3) * scale
    gain_in_out[...] = gain_total[0:1, :]
    gain_mid_out[...] = gain_total[1:3, :]
    proj_sum.zz()
    kernel_sum.xx()
    proj_sum.xx()
    kernel_sum.cc()
    proj_sum.cc()
    kernel_sum.end()
    for j in range(chans // 128):
        kernel_ref[:, j * 128 : (j + 1) * 128] = k_out[j * high : (j + 1) * high, :]
    proj_sum.end()
    high = wt_ref.shape[0]
    for j in range(width // 128):
        proj_ref[:, j * 128 : (j + 1) * 128] = p_out[j * high : (j + 1) * high, :]
    wire.drain()


def reduce_scratch(elements, over_y=0):
    rows = -(-elements // (128 * 32 * 16)) * 16
    lead = (over_y,) if over_y else ()
    shapes = [lead + (32 * rows, 128), lead + (16 * rows, 128), (16 * rows, 128)]
    shapes += [(3, 4 * rows, 128), (4 * rows, 128), (3, rows, 128), (32 * rows, 128)]
    if over_y:
        shapes += [(over_y, 16 * rows, 128), (over_y - 1, 16 * rows, 128)]
    return [pltpu.VMEM(shape, BF16) for shape in shapes]


def body(section_input, conv_kernel, qkv_weight, gain_in, gain_mid, qkv_cotangent):
    x = section_input[0]
    length, chans = x.shape
    half = length // 2
    width = 2 * chans
    shards = lax.axis_size("seq")
    own = conv_kernel.shape[2]
    high = qkv_weight.shape[1]
    scale = 1.0 / math.sqrt(lax.axis_size("dp") * shards * half)
    taps = jnp.transpose(conv_kernel, (0, 2, 1)).reshape(5 * own, chans)
    pad_rows = -(-5 * own // 256) * 256
    positions = shards * half
    column = positions // 4
    vmem = pl.BlockSpec(memory_space=pltpu.VMEM)
    gain_shape = (8, chans)
    copies = 176
    qkv, input_grad, kernel, proj, gain_in_grad, gain_mid_grad = pl.pallas_call(
        functools.partial(whole_kernel, scale, own),
        name="whole",
        out_shape=(
            jax.ShapeDtypeStruct((high, positions), BF16),
            jax.ShapeDtypeStruct((length, chans), BF16),
            jax.ShapeDtypeStruct((5 * own, chans), BF16),
            jax.ShapeDtypeStruct((high, width), BF16),
            jax.ShapeDtypeStruct((1, chans), F32),
            jax.ShapeDtypeStruct((2, chans), F32),
        ),
        in_specs=[vmem] * 5,
        out_specs=(vmem,) * 6,
        scratch_shapes=[
            pltpu.VMEM((4, length + 16, chans), BF16),
            pltpu.VMEM((5, 4 * length, chans), BF16),
            pltpu.VMEM((shards, pad_rows, chans), BF16),
            pltpu.VMEM((shards, half, width), BF16),
            pltpu.VMEM((4, 4 * own, length), BF16),
            pltpu.VMEM((length + 16, chans), F32),
            pltpu.VMEM((length + 16, chans), F32),
            pltpu.VMEM((length + 16, chans), F32),
            pltpu.VMEM((4, 8, chans), F32),
            pltpu.VMEM((5, length, chans), BF16),
            pltpu.VMEM((length, chans), F32),
            pltpu.VMEM((chans // 128, length, 128), F32),
            pltpu.VMEM((half, width), F32),
            pltpu.VMEM((half, 128), F32),
            pltpu.VMEM((chans // 128, length, 128), F32),
            pltpu.VMEM((length, chans), F32),
            pltpu.VMEM((chans, length), BF16),
            pltpu.VMEM((4, 4 * own, length), BF16),
            pltpu.VMEM((4, column, high), BF16),
            pltpu.VMEM((4, column, width), F32),
            pltpu.VMEM((column, width), BF16),
            pltpu.VMEM((2, column // 2, width), BF16),
            pltpu.VMEM((2, column, width), BF16),
            pltpu.VMEM((2, column, width), BF16),
            pltpu.VMEM((4, half, width), BF16),
            pltpu.VMEM((3, half, width), BF16),
            pltpu.VMEM((high, width), F32),
            *reduce_scratch(5 * own * chans, 4),
            *reduce_scratch(high * width),
            pltpu.VMEM(gain_shape, F32),
            pltpu.VMEM(gain_shape, F32),
            pltpu.VMEM((4,) + gain_shape, F32),
            pltpu.VMEM((4, 3) + gain_shape, F32),
            pltpu.SemaphoreType.DMA((copies,)),
            pltpu.SemaphoreType.DMA((copies,)),
        ],
        compiler_params=pltpu.CompilerParams(collective_id=0, has_side_effects=True, vmem_limit_bytes=60 << 20),
    )(x, taps, qkv_weight.T, qkv_cotangent[0].T, jnp.concatenate([gain_in, gain_mid]).reshape(3, chans))
    return (
        qkv.T[None],
        input_grad[None],
        jnp.transpose(kernel.reshape(5, own, chans), (0, 2, 1)),
        gain_in_grad.reshape(chans),
        gain_mid_grad.reshape(width),
        proj.T,
    )


def solution(mesh):
    placed = (
        P("dp", "seq", None),
        P(None, None, "seq"),
        P(None, "seq"),
        P(),
        P(),
        P("dp", None, "seq"),
    )
    return jax.shard_map(
        body,
        mesh=mesh,
        in_specs=placed,
        out_specs=(
            P("dp", None, "seq"),
            P("dp", "seq", None),
            P(None, None, "seq"),
            P(),
            P(),
            P(None, "seq"),
        ),
        check_vma=False,
    )
```

```python
import functools
import math

import jax
import jax.numpy as jnp
from jax import lax
from jax.experimental import pallas as pl
from jax.experimental.pallas import tpu as pltpu
from jax.sharding import PartitionSpec as P

EPS = 1e-06
MESH = pl.DeviceIdType.MESH
F32 = jnp.float32
BF16 = jnp.bfloat16


def wrap4(i):
    return lax.rem(i + 8, 4)


class Place:
    def __init__(self):
        self.dp = lax.axis_index("dp")
        self.seq = lax.axis_index("seq")
        self.z_hi = self.dp // 8
        self.x = lax.rem(self.dp // 2, 4)
        self.core = lax.rem(self.dp, 2)
        self.y = self.seq // 4
        self.z = lax.rem(self.seq, 4)

    def at_seq(self, y, z):
        return (self.dp, y * 4 + z)

    def y_peer(self, step):
        return self.at_seq(wrap4(self.y + step), self.z)

    def z_peer(self, step):
        return self.at_seq(self.y, wrap4(self.z + step))

    def x_peer(self, step):
        return (self.z_hi * 8 + wrap4(self.x + step) * 2 + self.core, self.seq)

    def z_hi_peer(self, step):
        return (wrap4(self.z_hi + step) * 8 + self.x * 2 + self.core, self.seq)

    def other_core(self):
        return (self.z_hi * 8 + self.x * 2 + 1 - self.core, self.seq)


class Wire:
    def __init__(self, send_sems, recv_sems, anyone):
        self.send_sems = send_sems
        self.recv_sems = recv_sems
        self.anyone = anyone
        self.started = []
        self.names = {}

    def number(self, name):
        return self.names.setdefault(name, len(self.names))

    def send(self, name, src, dst, device):
        k = self.number(name)
        copy = pltpu.make_async_remote_copy(
            src_ref=src,
            dst_ref=dst,
            send_sem=self.send_sems.at[k],
            recv_sem=self.recv_sems.at[k],
            device_id=device,
            device_id_type=MESH,
        )
        copy.start()
        self.started.append(copy)

    def recv(self, name, ref):
        k = self.number(name)
        pltpu.make_async_remote_copy(
            src_ref=ref,
            dst_ref=ref,
            send_sem=self.send_sems.at[k],
            recv_sem=self.recv_sems.at[k],
            device_id=self.anyone,
            device_id_type=MESH,
        ).wait_recv()

    def drain(self):
        for copy in self.started:
            copy.wait_send()


class Gather:
    order = (0, 1, 3, 2)

    def __init__(self, wire, place, tag, view):
        self.wire, self.place, self.tag, self.view = wire, place, tag, view

    def block(self, step, d):
        p = self.place
        return self.view(wrap4(p.y + step) * 4 + wrap4(p.z - d))

    def round_ring(self, d, src):
        for step in (1, -1):
            self.wire.send((self.tag, "y", step, d), src, self.block(0, d), self.place.y_peer(step))

    def line(self, ds, src):
        for d in ds:
            self.wire.send((self.tag, "z", d), src, self.block(0, 0), self.place.z_peer(d))

    def start(self, src):
        self.line((1, 3, 2), src)
        self.round_ring(0, src)

    def own(self, d):
        got = self.block(0, d)
        self.wire.recv((self.tag, "z", d), got)
        self.round_ring(d, got)

    def near(self, d):
        for step in (1, -1):
            got = self.block(-step, d)
            self.wire.recv((self.tag, "y", step, d), got)
            if (step == 1) == (d in (0, 1)):
                self.wire.send((self.tag, "relay", d), got, got, self.place.y_peer(step))

    def far(self, d):
        self.wire.recv((self.tag, "relay", d), self.block(2, d))


class Reduce:
    ways = (1, 3, 2)

    def __init__(self, wire, place, tag, rows, scale, packed, core_recv, core_sum, x_recv, x_sum, z_recv, out):
        self.wire, self.place, self.tag, self.rows, self.scale = wire, place, tag, rows, scale
        self.packed, self.core_recv, self.core_sum = packed, core_recv, core_sum
        self.x_recv, self.x_sum, self.z_recv, self.out = x_recv, x_sum, z_recv, out

    def span(self, blocks, count):
        return pl.ds(pl.multiple_of(blocks * self.rows, 16), count * self.rows)

    def core(self):
        p = self.place
        self.wire.send((self.tag, "core"), self.packed.at[self.span((1 - p.core) * 16, 16)], self.core_recv, p.other_core())

    def before_x(self):
        self.wire.recv((self.tag, "core"), self.core_recv)

    def chip_total(self, x):
        mine = self.packed[self.span(self.place.core * 16 + x * 4, 4), :].astype(F32)
        return mine + self.core_recv[self.span(x * 4, 4), :].astype(F32)

    def x(self):
        p = self.place
        self.before_x()

        def add(x):
            self.core_sum[self.span(x * 4, 4), :] = self.chip_total(x).astype(BF16)

        for d in self.ways:
            to = wrap4(p.x + d)
            add(to)
            self.wire.send((self.tag, "x", d), self.core_sum.at[self.span(to * 4, 4)], self.x_recv.at[d - 1], p.x_peer(d))
        add(p.x)

    def z(self):
        p = self.place
        for d in self.ways:
            self.wire.recv((self.tag, "x", d), self.x_recv.at[d - 1])

        def add(z):
            total = self.core_sum[self.span(p.x * 4 + z, 1), :].astype(F32)
            here = self.span(z, 1)
            for d in self.ways:
                total = total + self.x_recv[d - 1, here, :].astype(F32)
            self.x_sum[here, :] = total.astype(BF16)

        for d in (2, 1, 3):
            to = wrap4(p.z_hi + d)
            add(to)
            self.wire.send((self.tag, "z", d), self.x_sum.at[self.span(to, 1)], self.z_recv.at[d - 1], p.z_hi_peer(d))
        add(p.z_hi)

    def zz(self):
        p = self.place
        total = self.x_sum[self.span(p.z_hi, 1), :].astype(F32)
        for d in self.ways:
            self.wire.recv((self.tag, "z", d), self.z_recv.at[d - 1])
            total = total + self.z_recv[d - 1].astype(F32)
        here = self.span(p.core * 16 + p.x * 4 + p.z_hi, 1)
        self.out[here, :] = (total * self.scale).astype(BF16)
        mine = self.out.at[here]
        for d in (2, 1, 3):
            self.wire.send((self.tag, "zz", d), mine, mine, p.z_hi_peer(d))
        self.to_x(0)

    def final(self, core, dx, dz, count=1):
        p = self.place
        z = wrap4(p.z_hi - dz) if count == 1 else 0
        return self.out.at[self.span(core * 16 + wrap4(p.x - dx) * 4 + z, count)]

    def to_x(self, dz):
        p = self.place
        mine = self.final(p.core, 0, dz)
        for d in self.ways:
            self.wire.send((self.tag, "xx", d, dz), mine, mine, p.x_peer(d))

    def to_core(self, dx):
        mine = self.final(self.place.core, dx, 0, 4)
        self.wire.send((self.tag, "cc", dx), mine, mine, self.place.other_core())

    def xx(self):
        for dz in (1, 3, 2):
            self.wire.recv((self.tag, "zz", dz), self.final(self.place.core, 0, dz))
            self.to_x(dz)
        self.to_core(0)

    def cc(self):
        for dx in self.ways:
            for dz in (0, 1, 3, 2):
                self.wire.recv((self.tag, "xx", dx, dz), self.final(self.place.core, dx, dz))
            self.to_core(dx)

    def end(self):
        for dx in (0, 1, 3, 2):
            self.wire.recv((self.tag, "cc", dx), self.final(1 - self.place.core, dx, 0, 4))


class ReduceOverY(Reduce):
    def core(self):
        p = self.place
        theirs = self.packed.at[:, self.span((1 - p.core) * 16, 16)]
        self.wire.send((self.tag, "core"), theirs, self.core_recv, p.other_core())

    def y(self, sums, got):
        p = self.place
        self.y_sums, self.y_got = sums, got
        self.wire.recv((self.tag, "core"), self.core_recv)

        def add(y):
            mine = self.packed[y, self.span(p.core * 16, 16), :].astype(F32)
            sums[y] = (mine + self.core_recv[y].astype(F32)).astype(BF16)

        for d in self.ways:
            to = wrap4(p.y + d)
            add(to)
            self.wire.send((self.tag, "y", d), sums.at[to], got.at[d - 1], p.y_peer(d))
        add(p.y)

    def before_x(self):
        for d in self.ways:
            self.wire.recv((self.tag, "y", d), self.y_got.at[d - 1])

    def chip_total(self, x):
        here = self.span(x * 4, 4)
        total = self.y_sums[self.place.y, here, :].astype(F32)
        for d in range(3):
            total = total + self.y_got[d, here, :].astype(F32)
        return total


class GainSum:
    ways = (1, 3, 2)

    def __init__(self, wire, place, core_recv, held, got):
        self.wire, self.core_recv, self.held, self.got = wire, core_recv, held, got
        self.place = place
        self.peers = (place.x_peer, place.z_hi_peer, place.z_peer, place.y_peer)

    def start(self, src):
        self.wire.send("gain", src, self.core_recv, self.place.other_core())

    def spread(self, stage):
        for d in self.ways:
            self.wire.send(("gain", stage, d), self.held.at[stage], self.got.at[stage, d - 1], self.peers[stage](d))

    def total(self, stage):
        value = self.held[stage]
        for d in self.ways:
            self.wire.recv(("gain", stage, d), self.got.at[stage, d - 1])
            value = value + self.got[stage, d - 1]
        return value

    def first(self, src):
        self.wire.recv("gain", self.core_recv)
        self.held[0] = src[...] + self.core_recv[...]
        self.spread(0)

    def onward(self, stage):
        self.held[stage] = self.total(stage - 1)
        self.spread(stage)


def contract(a, b, dims):
    return lax.dot_general(a, b, (dims, ((), ())), preferred_element_type=F32)


def whole_kernel(
    scale, own, x_ref, taps_ref, wt_ref, cot_ref, gain_ref,
    qkv_ref, input_grad_ref, kernel_ref, proj_ref, gain_in_out, gain_mid_out,
    line_rows, line_shifted, all_taps, all_mid, all_cols, slab,
    ext, ext_back, halo, shifted, conv, section, atwo, rtwo, section_grad, normed_grad, cols, cols_by_z,
    part, sums, far_send, far_recv, near_send, near_recv, column_send, z_recv,
    pacc,
    k_packed, k_core, k_csum, k_x, k_xsum, k_z, k_out, k_ysum, k_y,
    p_packed, p_core, p_csum, p_x, p_xsum, p_z, p_out,
    g_own, g_core, g_held, g_got,
    send_sems, recv_sems,
):
    p = Place()
    wire = Wire(send_sems, recv_sems, p.other_core())
    length, chans = x_ref.shape
    half = length // 2
    width = 2 * chans
    shards = all_mid.shape[0]
    nlast = shards - 1

    def seq_peer(d):
        return (p.dp, lax.rem(p.seq + d, shards))

    peers = [seq_peer(1), seq_peer(nlast), p.other_core()]
    peers += [peer(d) for peer in (p.x_peer, p.y_peer, p.z_peer, p.z_hi_peer) for d in (1, 2, 3)]
    own_rows, pad_rows = taps_ref.shape[0], all_taps.shape[1]
    all_taps[p.seq, 0:own_rows, :] = taps_ref[...]
    all_taps[p.seq, own_rows:pad_rows, :] = jnp.zeros((pad_rows - own_rows, chans), BF16)
    barrier = pltpu.get_barrier_semaphore()
    for peer in peers:
        pl.semaphore_signal(barrier, inc=1, device_id=peer, device_id_type=MESH)

    step_rows = 32

    def chunks(body, count=length, size=step_rows):
        @pl.loop(0, count // size)
        def _(i):
            body(pl.multiple_of(i * size, size))

    def first_norm(at, size=step_rows):
        x = x_ref[pl.ds(at, size), :].astype(F32)
        r = lax.rsqrt(jnp.mean(x * x, axis=-1, keepdims=True) + EPS)
        return x, r, x * r

    def norm_rows(at):
        normed = (first_norm(at)[2] * gain_ref[0:1, :]).astype(BF16)
        ext[pl.ds(8 + at, step_rows), :] = normed.astype(F32)

    chunks(norm_rows)
    pl.semaphore_wait(barrier, len(peers))

    lanes_half = chans // 2
    whole_rows = pad_rows // 4
    quarter = (pad_rows - whole_rows) // 4

    def core_lanes(core):
        return pl.ds(pl.multiple_of(core * lanes_half, 128), lanes_half)

    def piece(x):
        return pl.ds(pl.multiple_of(whole_rows + x * quarter, 16), quarter)

    my_lanes = core_lanes(p.core)
    taps_part = Gather(wire, p, "part", lambda block: all_taps.at[block, piece(p.x), my_lanes])
    taps_whole = Gather(wire, p, "whole", lambda block: all_taps.at[block, pl.ds(0, whole_rows), my_lanes])
    mid_rows = half // 2
    mids = [
        Gather(wire, p, ("mid", i), lambda block, i=i: all_mid.at[block, pl.ds(i * mid_rows, mid_rows)])
        for i in range(2)
    ]
    for taps in (taps_part, taps_whole):
        taps.start(taps.block(0, 0))
    wire.send("tail", ext.at[pl.ds(length, 8)], halo.at[0], seq_peer(1))
    wire.send("head", ext.at[pl.ds(8, 8)], halo.at[1], seq_peer(nlast))

    def x_part(x, column):
        return all_taps.at[pl.ds(wrap4(p.y + column) * 4, 4), piece(x), my_lanes]

    def x_send(column):
        mine = x_part(p.x, column)
        for way in (1, -1):
            wire.send(("x", way, column), mine, mine, p.x_peer(way))

    def x_relay(column):
        for way in (1, -1):
            got = x_part(wrap4(p.x - way), column)
            wire.recv(("x", way, column), got)
            if (way == 1) == (column in (0, 1)):
                wire.send(("xx", column), got, got, p.x_peer(way))

    def core_part(core, column):
        return all_taps.at[pl.ds(wrap4(p.y + column) * 4, 4), :, core_lanes(core)]

    def core_send(column):
        wire.recv(("xx", column), x_part(wrap4(p.x + 2), column))
        mine = core_part(p.core, column)
        wire.send(("core", column), mine, mine, p.other_core())

    span_rows = cot_ref.shape[1] // 4
    span_half = span_rows // 2
    tile = 256
    slot_of = {2: 0, 1: 1, -1: 2, 0: 3}

    def column_lanes(step):
        return pl.ds(pl.multiple_of(wrap4(p.y + step) * span_rows, 128), span_rows)

    def half_lanes(h):
        return pl.ds(h * chans, chans)

    def product(step, h):
        if h == 0:
            part[slot_of[step]] = cot_ref[:, column_lanes(step)].T

        @pl.loop(0, chans // tile)
        def _(n):
            span = pl.ds(pl.multiple_of(h * chans + n * tile, tile), tile)
            sums[slot_of[step], :, span] = contract(part[slot_of[step]], wt_ref[:, span], ((1,), (0,)))

    def far_out(h):
        lanes = half_lanes(h)
        far_send[:, lanes] = sums[0, :, lanes].astype(BF16)
        wire.send(("far+", h), far_send.at[pl.ds(0, span_half), lanes], far_recv.at[0, :, lanes], p.y_peer(1))
        wire.send(("far-", h), far_send.at[pl.ds(span_half, span_half), lanes], far_recv.at[1, :, lanes], p.y_peer(-1))

    def near_out(h):
        lanes = half_lanes(h)
        wire.recv(("far+", h), far_recv.at[0, :, lanes])
        near_send[0, :span_half, lanes] = (sums[1, :span_half, lanes] + far_recv[0, :, lanes].astype(F32)).astype(BF16)
        near_send[0, span_half:, lanes] = sums[1, span_half:, lanes].astype(BF16)
        wire.send(("near+", h), near_send.at[0, :, lanes], near_recv.at[0, :, lanes], p.y_peer(1))
        wire.recv(("far-", h), far_recv.at[1, :, lanes])
        near_send[1, :span_half, lanes] = sums[2, :span_half, lanes].astype(BF16)
        near_send[1, span_half:, lanes] = (sums[2, span_half:, lanes] + far_recv[1, :, lanes].astype(F32)).astype(BF16)
        wire.send(("near-", h), near_send.at[1, :, lanes], near_recv.at[1, :, lanes], p.y_peer(-1))

    def mid_out(h):
        lanes = half_lanes(h)
        wire.recv(("near+", h), near_recv.at[0, :, lanes])
        wire.recv(("near-", h), near_recv.at[1, :, lanes])

        @pl.loop(0, 4)
        def _(i):
            at = pl.ds(pl.multiple_of(i * half, 16), half)
            total = sums[3, at, lanes] + near_recv[0, at, lanes].astype(F32) + near_recv[1, at, lanes].astype(F32)
            sums[3, at, lanes] = total
            column_send[i, :, lanes] = total.astype(BF16)

        for d in (1, 3, 2):
            wire.send(("mid", h, d), column_send.at[wrap4(p.z + d), :, lanes], z_recv.at[d - 1, :, lanes], p.z_peer(d))

    def mid_in(h):
        for d in (1, 3, 2):
            wire.recv(("mid", h, d), z_recv.at[d - 1, :, half_lanes(h)])

    def edges(into, recv):
        into[0:8, :] = jnp.where(p.seq > 0, recv[0], 0.0)
        into[length + 8 : length + 16, :] = jnp.where(p.seq < nlast, recv[1], 0.0)

    product(2, 0)
    far_out(0)
    product(2, 1)
    for d in (1, 3, 2):
        taps_part.own(d)
    x_send(0)
    for d in (1, 3, 2):
        taps_whole.own(d)
    wire.recv("tail", halo.at[0])
    wire.recv("head", halo.at[1])
    edges(ext, halo)
    line_rows[p.z] = ext[...].astype(BF16)
    for d in (1, 3, 2):
        wire.send(("rows", d), line_rows.at[p.z], line_rows.at[p.z], p.z_peer(d))
    for d in taps_part.order:
        taps_part.near(d)
    x_send(1)
    x_send(-1)
    for d in taps_whole.order:
        taps_whole.near(d)
    product(1, 0)
    product(-1, 0)
    near_out(0)
    far_out(1)
    for d in taps_part.order:
        taps_part.far(d)
    x_send(2)
    product(1, 1)
    product(-1, 1)
    x_relay(0)
    product(0, 0)
    product(0, 1)
    for d in taps_whole.order:
        taps_whole.far(d)
    for k in range(5):
        shifted[k] = ext[6 + k : 6 + k + length, :].astype(BF16)
    x_relay(1)
    x_relay(-1)
    x_relay(2)
    core_send(0)
    core_send(1)
    mid_out(0)
    core_send(-1)
    core_send(2)
    near_out(1)
    for column in (0, 1, -1, 2):
        wire.recv(("core", column), core_part(1 - p.core, column))

    def taps_of(k, group, lanes=slice(None)):
        block = all_taps[group * (shards // 2) : (group + 1) * (shards // 2), k * own : (k + 1) * own, lanes]
        return block.reshape(lanes_half, -1)

    for group in range(2):
        total = contract(shifted[0], taps_of(0, group), ((1,), (1,)))
        for k in range(1, 5):
            total = total + contract(shifted[k], taps_of(k, group), ((1,), (1,)))
        conv[:, group * lanes_half : (group + 1) * lanes_half] = total

    def section_rows(at):
        here = pl.ds(at, step_rows)
        c = conv[here, :]
        value = x_ref[here, :].astype(F32) + c * jax.nn.sigmoid(c)
        for j in range(chans // 128):
            section[j, here, :] = value[:, j * 128 : (j + 1) * 128]

    chunks(section_rows)
    pool_rows = 16

    def pool(i):
        at = i * pool_rows
        here = slice(at, at + pool_rows)
        even, odd = (
            jnp.concatenate(
                [section[j, pl.ds(2 * at + i, pool_rows, stride=2), :] for j in range(chans // 128)], axis=1
            )
            for i in range(2)
        )
        squares = jnp.sum(even * even, axis=-1, keepdims=True) + jnp.sum(odd * odd, axis=-1, keepdims=True)
        r = lax.rsqrt(squares / width + EPS)
        rtwo[here, :] = jnp.broadcast_to(r, (pool_rows, 128))
        for j, value in enumerate((even * r, odd * r)):
            lanes = slice(j * chans, (j + 1) * chans)
            atwo[here, lanes] = value
            all_mid[p.seq, here, lanes] = (value * gain_ref[1 + j : 2 + j, :]).astype(BF16)

    for i in range(half // pool_rows):
        pool(i)
    for mid in mids:
        mid.round_ring(0, mid.block(0, 0))
        mid.line((1, 3), mid.block(0, 0))
    mid_out(1)
    for mid in mids:
        mid.line((2,), mid.block(0, 0))
    for d in (1, 3, 2):
        wire.recv(("rows", d), line_rows.at[wrap4(p.z - d)])

    @pl.loop(0, 4)
    def _(z):
        slab[...] = line_rows[z].astype(F32)
        for k in range(5):
            at = pl.ds(pl.multiple_of(z * length, 128), length)
            line_shifted[k, at, :] = slab[6 + k : 6 + k + length, :].astype(BF16)

    for mid in mids:
        mid.own(1)
    for mid in mids:
        mid.own(3)
    for d in (0, 1, 3):
        for mid in mids:
            mid.near(d)

    mid_in(0)
    mid_in(1)
    g_own[...] = jnp.zeros_like(g_own)

    def pool_back(i):
        at = i * pool_rows
        here = slice(at, at + pool_rows)
        r = rtwo[here, 0:1]
        grads, terms = [], 0.0
        for j in range(2):
            lanes = slice(j * chans, (j + 1) * chans)
            there = pl.ds(pl.multiple_of(p.z * half + at, 16), pool_rows)
            grad = sums[3, there, lanes]
            for d in range(3):
                grad = grad + z_recv[d, here, lanes].astype(F32)
            a = atwo[here, lanes]
            g_own[1 + j : 2 + j, :] += jnp.sum(grad * a, axis=0, keepdims=True)
            g = gain_ref[1 + j : 2 + j, :] * grad
            terms = terms + jnp.sum(g * a, axis=-1, keepdims=True)
            grads.append((g, a))
        for j, (g, a) in enumerate(grads):
            value = r * (g - a * (terms / width))
            for n in range(chans // 128):
                section_grad[n, pl.ds(2 * at + j, pool_rows, stride=2), :] = value[:, n * 128 : (n + 1) * 128]

    def section_grad_rows(here):
        return jnp.concatenate([section_grad[n, here, :] for n in range(chans // 128)], axis=1)

    for i in range(half // pool_rows):
        pool_back(i)

    def conv_back(at):
        here = pl.ds(at, step_rows)
        c = conv[here, :]
        s = jax.nn.sigmoid(c)
        grad = section_grad_rows(here) * s * (1.0 + c * (1.0 - s))
        ext_back[pl.ds(8 + at, step_rows), :] = grad.astype(BF16).astype(F32)

    chunks(conv_back)
    wire.send("tail back", ext_back.at[pl.ds(length, 8)], halo.at[2], seq_peer(1))
    wire.send("head back", ext_back.at[pl.ds(8, 8)], halo.at[3], seq_peer(nlast))
    for j in range(chans // 128):
        lanes = slice(j * 128, (j + 1) * 128)
        cols[lanes, :] = ext_back[8 : 8 + length, lanes].T.astype(BF16)

    for z in range(4):
        for y in range(4):
            block = 4 * y + z
            cols_by_z[z, y * own : (y + 1) * own, :] = cols[block * own : (block + 1) * own, :]
    for d in (1, 3, 2):
        wire.send(("cols", d), cols_by_z.at[wrap4(p.z + d)], all_cols.at[p.z], p.z_peer(d))
    all_cols[p.z] = cols_by_z[p.z]
    mids[0].own(2)

    wire.recv("tail back", halo.at[2])
    wire.recv("head back", halo.at[3])
    edges(ext_back, halo.at[pl.ds(2, 2)])
    for k in range(5):
        shifted[k] = ext_back[10 - k : 10 - k + length, :].astype(BF16)

    def through(n):
        lanes = slice(n * lanes_half, (n + 1) * lanes_half)
        total = None
        for k in range(5):
            for group in range(2):
                left = shifted[k, :, group * lanes_half : (group + 1) * lanes_half]
                term = contract(left, taps_of(k, group, lanes), ((1,), (0,)))
                total = term if total is None else total + term
        normed_grad[:, lanes] = total

    def qkv_of(step):
        block = all_mid[pl.ds(wrap4(p.y + step) * 4, 4)].reshape(span_rows, width)
        qkv_ref[:, column_lanes(step)] = contract(wt_ref[...], block, ((1,), (1,))).astype(BF16)

    def project(step, last=False):
        left = cot_ref[:, column_lanes(step)]
        for n in range(width // tile):
            span = slice(n * tile, (n + 1) * tile)
            term = contract(left, all_mid[pl.ds(wrap4(p.y + step) * 4, 4), :, span].reshape(span_rows, tile), ((1,), (0,)))
            if step != 0:
                term = term + pacc[:, span]
            if last:
                high = term.shape[0]
                for j in range(tile // 128):
                    at = (n * (tile // 128) + j) * high
                    p_packed[at : at + high, :] = term[:, j * 128 : (j + 1) * 128].astype(BF16)
            else:
                pacc[:, span] = term

    through(0)
    mids[1].own(2)
    through(1)

    def last_rows(at):
        here = pl.ds(at, step_rows)
        _, r, a = first_norm(at)
        grad = normed_grad[here, :]
        h = gain_ref[0:1, :] * grad
        g_own[0:1, :] += jnp.sum(grad * a, axis=0, keepdims=True)
        mean = jnp.mean(h * a, axis=-1, keepdims=True)
        input_grad_ref[here, :] = (section_grad_rows(here) + r * (h - a * mean)).astype(BF16)

    chunks(last_rows)
    gains = GainSum(wire, p, g_core, g_held, g_got)
    gains.start(g_own)

    for mid in mids:
        mid.near(2)

    for d in (1, 3, 2):
        wire.recv(("cols", d), all_cols.at[wrap4(p.z - d)])
    left = jnp.concatenate([all_cols[z] for z in range(4)], axis=1)
    high = 5 * own
    for k in range(5):
        for n in range(chans // tile):
            term = contract(left, line_shifted[k, :, n * tile : (n + 1) * tile], ((1,), (0,)))
            for j in range(tile // 128):
                at = (n * (tile // 128) + j) * high + k * own
                for y in range(4):
                    value = term[y * own : (y + 1) * own, j * 128 : (j + 1) * 128]
                    k_packed[y, at : at + own, :] = value.astype(BF16)

    def zero_rest(packed, used):
        packed[used:, :] = jnp.zeros((packed.shape[0] - used, 128), BF16)

    for y in range(4):
        zero_rest(k_packed.at[y], high * (chans // 128))
    zero_rest(p_packed, wt_ref.shape[0] * (width // 128))
    kernel_sum = ReduceOverY(wire, p, "k", k_z.shape[1], scale, k_packed, k_core, k_csum, k_x, k_xsum, k_z, k_out)
    proj_sum = Reduce(wire, p, "p", p_z.shape[1], scale, p_packed, p_core, p_csum, p_x, p_xsum, p_z, p_out)
    kernel_sum.core()
    gains.first(g_own)
    kernel_sum.y(k_ysum, k_y)
    project(0)
    project(1)
    project(-1)
    gains.onward(1)
    for mid in mids:
        for d in mid.order:
            mid.far(d)
    project(2, last=True)
    proj_sum.core()
    qkv_of(0)
    proj_sum.x()
    kernel_sum.x()
    gains.onward(2)
    qkv_of(1)
    proj_sum.z()
    kernel_sum.z()
    qkv_of(-1)
    qkv_of(2)
    proj_sum.zz()
    gains.onward(3)
    kernel_sum.zz()
    proj_sum.xx()
    kernel_sum.xx()
    gain_total = gains.total(3) * scale
    gain_in_out[...] = gain_total[0:1, :]
    gain_mid_out[...] = gain_total[1:3, :]
    proj_sum.cc()
    kernel_sum.cc()
    proj_sum.end()
    proj_rows = wt_ref.shape[0]
    for j in range(width // 128):
        proj_ref[:, j * 128 : (j + 1) * 128] = p_out[j * proj_rows : (j + 1) * proj_rows, :]
    kernel_sum.end()
    for j in range(chans // 128):
        kernel_ref[:, j * 128 : (j + 1) * 128] = k_out[j * high : (j + 1) * high, :]
    wire.drain()


def reduce_scratch(elements, over_y=0):
    rows = -(-elements // (128 * 32 * 16)) * 16
    lead = (over_y,) if over_y else ()
    shapes = [lead + (32 * rows, 128), lead + (16 * rows, 128), (16 * rows, 128)]
    shapes += [(3, 4 * rows, 128), (4 * rows, 128), (3, rows, 128), (32 * rows, 128)]
    if over_y:
        shapes += [(over_y, 16 * rows, 128), (over_y - 1, 16 * rows, 128)]
    return [pltpu.VMEM(shape, BF16) for shape in shapes]


def body(section_input, conv_kernel, qkv_weight, gain_in, gain_mid, qkv_cotangent):
    x = section_input[0]
    length, chans = x.shape
    half = length // 2
    width = 2 * chans
    shards = lax.axis_size("seq")
    own = conv_kernel.shape[2]
    high = qkv_weight.shape[1]
    scale = 1.0 / math.sqrt(lax.axis_size("dp") * shards * half)
    taps = jnp.transpose(conv_kernel, (0, 2, 1)).reshape(5 * own, chans)
    pad_rows = -(-5 * own // 256) * 256
    positions = shards * half
    column = positions // 4
    vmem = pl.BlockSpec(memory_space=pltpu.VMEM)
    gain_shape = (8, chans)
    copies = 176
    qkv, input_grad, kernel, proj, gain_in_grad, gain_mid_grad = pl.pallas_call(
        functools.partial(whole_kernel, scale, own),
        name="whole",
        out_shape=(
            jax.ShapeDtypeStruct((high, positions), BF16),
            jax.ShapeDtypeStruct((length, chans), BF16),
            jax.ShapeDtypeStruct((5 * own, chans), BF16),
            jax.ShapeDtypeStruct((high, width), BF16),
            jax.ShapeDtypeStruct((1, chans), F32),
            jax.ShapeDtypeStruct((2, chans), F32),
        ),
        in_specs=[vmem] * 5,
        out_specs=(vmem,) * 6,
        scratch_shapes=[
            pltpu.VMEM((4, length + 16, chans), BF16),
            pltpu.VMEM((5, 4 * length, chans), BF16),
            pltpu.VMEM((shards, pad_rows, chans), BF16),
            pltpu.VMEM((shards, half, width), BF16),
            pltpu.VMEM((4, 4 * own, length), BF16),
            pltpu.VMEM((length + 16, chans), F32),
            pltpu.VMEM((length + 16, chans), F32),
            pltpu.VMEM((length + 16, chans), F32),
            pltpu.VMEM((4, 8, chans), F32),
            pltpu.VMEM((5, length, chans), BF16),
            pltpu.VMEM((length, chans), F32),
            pltpu.VMEM((chans // 128, length, 128), F32),
            pltpu.VMEM((half, width), F32),
            pltpu.VMEM((half, 128), F32),
            pltpu.VMEM((chans // 128, length, 128), F32),
            pltpu.VMEM((length, chans), F32),
            pltpu.VMEM((chans, length), BF16),
            pltpu.VMEM((4, 4 * own, length), BF16),
            pltpu.VMEM((4, column, high), BF16),
            pltpu.VMEM((4, column, width), F32),
            pltpu.VMEM((column, width), BF16),
            pltpu.VMEM((2, column // 2, width), BF16),
            pltpu.VMEM((2, column, width), BF16),
            pltpu.VMEM((2, column, width), BF16),
            pltpu.VMEM((4, half, width), BF16),
            pltpu.VMEM((3, half, width), BF16),
            pltpu.VMEM((high, width), F32),
            *reduce_scratch(5 * own * chans, 4),
            *reduce_scratch(high * width),
            pltpu.VMEM(gain_shape, F32),
            pltpu.VMEM(gain_shape, F32),
            pltpu.VMEM((4,) + gain_shape, F32),
            pltpu.VMEM((4, 3) + gain_shape, F32),
            pltpu.SemaphoreType.DMA((copies,)),
            pltpu.SemaphoreType.DMA((copies,)),
        ],
        compiler_params=pltpu.CompilerParams(collective_id=0, has_side_effects=True, vmem_limit_bytes=60 << 20),
    )(x, taps, qkv_weight.T, qkv_cotangent[0].T, jnp.concatenate([gain_in, gain_mid]).reshape(3, chans))
    return (
        qkv.T[None],
        input_grad[None],
        jnp.transpose(kernel.reshape(5, own, chans), (0, 2, 1)),
        gain_in_grad.reshape(chans),
        gain_mid_grad.reshape(width),
        proj.T,
    )


def solution(mesh):
    placed = (
        P("dp", "seq", None),
        P(None, None, "seq"),
        P(None, "seq"),
        P(),
        P(),
        P("dp", None, "seq"),
    )
    return jax.shard_map(
        body,
        mesh=mesh,
        in_specs=placed,
        out_specs=(
            P("dp", None, "seq"),
            P("dp", "seq", None),
            P(None, None, "seq"),
            P(),
            P(),
            P(None, "seq"),
        ),
        check_vma=False,
    )
```
